128 devices in a mesh: grp: 8 (over z, core), tp: 16 (over x, y).
Axes of the slice: x: 4, y: 4, z: 4, core: 2. Of those that a mesh axis runs over, the one named last changes fastest.
Arguments:
- tokens: bfloat16 [4096, 4096], P('grp', 'tp'), may hold values from -6 to 6
- token_tenant: int32 [4096], P('grp'), may hold values from 0 to 63, as said below
- tenant_storage_slot: int32 [64], replicated, may hold values from 0 to 63, as said below
- gate_matrix: bfloat16 [4096, 14336], P(None, 'tp'), may hold values from -0.09375 to 0.09375
- up_matrix: bfloat16 [4096, 14336], P(None, 'tp'), may hold values from -0.09375 to 0.09375
- down_matrix: bfloat16 [14336, 4096], P('tp'), may hold values from -0.046875 to 0.046875
- adapter_gate_up_inputs: bfloat16 [64, 4096, 128], P('grp', 'tp'), may hold values from -0.09375 to 0.09375
- adapter_gate_up_outputs: bfloat16 [64, 128, 14336], P('grp', None, 'tp'), may hold values from -0.75 to 0.75
- adapter_down_inputs: bfloat16 [64, 14336, 64], P('grp', 'tp'), may hold values from -0.046875 to 0.046875
- adapter_down_outputs: bfloat16 [64, 64, 4096], P('grp', None, 'tp'), may hold values from -0.75 to 0.75
Outputs:
- mixed: bfloat16 [4096, 4096], P('grp', 'tp')
The draws below stay inside these ranges and needn't reach their ends.
Inputs may be any that keep to these rules, and one draw needn't show every extreme that they name: `token_tenant`: within each aligned block of 512 tokens, at most 128 tokens have tenants whose slot lies in one storage block of 8 slots; one storage block, chosen from the seed, receives exactly 128 tokens from every such block. `tenant_storage_slot`: A permutation of the tenants.
All inputs are finite; a program needn't handle non-finite values.
Results may differ from the reference program's by a relative error of at most 0.017.
Values may be sent and summed in bfloat16 or wider, within the bound.
No kernel may reach another device: no remote copies, remote signals or barrier semaphores. Data moves between devices by JAX's collectives and lax.ppermute only.
A program may use at most 128 MiB of HBM per device.

```python
import jax
import jax.numpy as jnp
from jax import lax

MODEL_WIDTH = 4096
HIDDEN_UNITS = 14336
ADAPTER_RANK = 64
TENANT_COUNT = 64
TOK_G = 512
TOKENS = 4096
TENANTS_PER_BLOCK = 8
CAP = 128
N_GRP = 8


def routing(key):
    home = jax.random.permutation(jax.random.fold_in(key, 11), TENANT_COUNT).astype(jnp.int32)
    hot = jax.random.randint(jax.random.fold_in(key, 12), (), 0, N_GRP).astype(jnp.int32)
    group_keys = jax.random.split(jax.random.fold_in(key, 13), N_GRP)

    def one_group(group_key):
        first_key, second_key = jax.random.split(group_key)
        ranks = jax.random.permutation(first_key, TOK_G).astype(jnp.int32)
        spread = (ranks - CAP) % (N_GRP - 1)
        other = spread + (spread >= hot).astype(jnp.int32)
        server = jnp.where(ranks < CAP, hot, other)
        local = jax.random.randint(second_key, (TOK_G,), 0, TENANTS_PER_BLOCK).astype(jnp.int32)
        return server * TENANTS_PER_BLOCK + local
    slots = jax.vmap(one_group)(group_keys).reshape(-1)
    owner = jnp.argsort(home).astype(jnp.int32)
    tenant = owner[slots].astype(jnp.int32)
    return (tenant, home)


def draw_token_tenant(key, part):
    return routing(key)[0]


def draw_tenant_storage_slot(key, part):
    return routing(key)[1]


def steps_of(rng, extent, shards, low, high):
    gain, own = 1.0, jax.random.fold_in(rng, 6)
    for dim, shards_of in shards:
        draws = jnp.exp(jax.random.uniform(jax.random.fold_in(own, dim), (shards_of,), jnp.float32, low / len(shards), high / len(shards)))
        gain = gain * jnp.repeat(draws, extent[dim] // shards_of).reshape([-1 if axis == dim else 1 for axis in range(len(extent))])
    return gain


def bell_draw(stream_key, shape, scale, reach, shards=(), kind=jnp.bfloat16):
    values = jax.random.normal(stream_key, shape, jnp.float32) * scale
    if len(shards) > 0:
        values = steps_of(stream_key, shape, shards, -0.22, 0.18) * values
    return jnp.clip(values, min=-reach, max=reach).astype(kind)


def setup_inputs(seed: int = 0) -> dict:
    splits = jax.random.split(jax.random.key(seed), 11)
    return {
        "tokens": bell_draw(splits[0], (TOKENS, MODEL_WIDTH), 1.0, 6.0, ((0, 8), (1, 16))),
        "token_tenant": draw_token_tenant(jax.random.fold_in(splits[10], 71), 0),
        "tenant_storage_slot": draw_tenant_storage_slot(jax.random.fold_in(splits[10], 71), 0),
        "gate_matrix": bell_draw(splits[3], (MODEL_WIDTH, HIDDEN_UNITS), MODEL_WIDTH ** -0.5, 0.09375, ((1, 16),)),
        "up_matrix": bell_draw(splits[4], (MODEL_WIDTH, HIDDEN_UNITS), MODEL_WIDTH ** -0.5, 0.09375, ((1, 16),)),
        "down_matrix": bell_draw(splits[5], (HIDDEN_UNITS, MODEL_WIDTH), HIDDEN_UNITS ** -0.5, 0.046875, ((0, 16),)),
        "adapter_gate_up_inputs": bell_draw(splits[6], (TENANT_COUNT, MODEL_WIDTH, 2 * ADAPTER_RANK), MODEL_WIDTH ** -0.5, 0.09375, ((0, 8), (1, 16))),
        "adapter_gate_up_outputs": bell_draw(splits[7], (TENANT_COUNT, 2 * ADAPTER_RANK, HIDDEN_UNITS), ADAPTER_RANK ** -0.5, 0.75, ((0, 8), (2, 16))),
        "adapter_down_inputs": bell_draw(splits[8], (TENANT_COUNT, HIDDEN_UNITS, ADAPTER_RANK), HIDDEN_UNITS ** -0.5, 0.046875, ((0, 8), (1, 16))),
        "adapter_down_outputs": bell_draw(splits[9], (TENANT_COUNT, ADAPTER_RANK, MODEL_WIDTH), ADAPTER_RANK ** -0.5, 0.75, ((0, 8), (2, 16))),
    }


def expand(onehot, vec):
    wide = onehot[:, :, None] * vec.astype(jnp.float32)[:, None, :]
    return wide.reshape(vec.shape[0], -1).astype(jnp.bfloat16)


def reference(tokens, token_tenant, tenant_storage_slot, gate_matrix, up_matrix, down_matrix, adapter_gate_up_inputs, adapter_gate_up_outputs, adapter_down_inputs, adapter_down_outputs):
    slot = tenant_storage_slot[token_tenant].astype(jnp.int32)
    server = slot // TENANTS_PER_BLOCK
    local = slot - server * TENANTS_PER_BLOCK
    width = N_GRP * CAP
    order = jnp.argsort(server, stable=True).astype(jnp.int32)
    counts = jnp.sum((server[:, None] == jnp.arange(N_GRP, dtype=jnp.int32)[None, :]).astype(jnp.int32), 0)
    starts = (jnp.cumsum(counts) - counts).astype(jnp.int32)
    padded = jnp.concatenate([order, jnp.zeros((width,), jnp.int32)])
    lanes = jnp.arange(TENANTS_PER_BLOCK, dtype=jnp.int32)

    def select(storage_block):
        picked = lax.dynamic_slice(padded, (starts[storage_block],), (width,))
        live = jnp.arange(width, dtype=jnp.int32) < counts[storage_block]
        onehot = jnp.where(live[:, None] & (local[picked][:, None] == lanes[None, :]), 1.0, 0.0).astype(jnp.float32)
        return picked, live, onehot

    def gate_up_step(carry, storage_block):
        total_gate, total_up = carry
        picked, live, onehot = select(storage_block)
        input_factor = lax.dynamic_slice_in_dim(adapter_gate_up_inputs, storage_block * TENANTS_PER_BLOCK, TENANTS_PER_BLOCK, 0)
        output_factor = lax.dynamic_slice_in_dim(adapter_gate_up_outputs, storage_block * TENANTS_PER_BLOCK, TENANTS_PER_BLOCK, 0)
        rows = tokens[picked].astype(jnp.float32)
        part = jnp.einsum('ny,eyq->neq', rows, input_factor.astype(jnp.float32))
        ranks = jnp.sum(part * onehot[:, :, None], 1).astype(jnp.bfloat16)
        gate_output_factor = output_factor[:, :ADAPTER_RANK, :].reshape(TENANTS_PER_BLOCK * ADAPTER_RANK, HIDDEN_UNITS)
        up_output_factor = output_factor[:, ADAPTER_RANK:, :].reshape(TENANTS_PER_BLOCK * ADAPTER_RANK, HIDDEN_UNITS)
        delta_gate = jnp.dot(expand(onehot, ranks[:, :ADAPTER_RANK]), gate_output_factor, preferred_element_type=jnp.float32).astype(jnp.bfloat16)
        delta_up = jnp.dot(expand(onehot, ranks[:, ADAPTER_RANK:]), up_output_factor, preferred_element_type=jnp.float32).astype(jnp.bfloat16)
        zero = jnp.zeros((), jnp.bfloat16)
        total_gate = total_gate.at[picked].add(jnp.where(live[:, None], delta_gate, zero))
        total_up = total_up.at[picked].add(jnp.where(live[:, None], delta_up, zero))
        return (total_gate, total_up), None

    empty = jnp.zeros((TOKENS, HIDDEN_UNITS), jnp.bfloat16)
    blocks = jnp.arange(N_GRP, dtype=jnp.int32)
    (delta_gate, delta_up), _ = lax.scan(gate_up_step, (empty, empty), blocks)
    gate = jnp.dot(tokens, gate_matrix, preferred_element_type=jnp.float32) + delta_gate.astype(jnp.float32)
    up = jnp.dot(tokens, up_matrix, preferred_element_type=jnp.float32) + delta_up.astype(jnp.float32)
    hidden = (jax.nn.silu(gate) * up).astype(jnp.bfloat16)

    def down_step(total, storage_block):
        picked, live, onehot = select(storage_block)
        input_factor = lax.dynamic_slice_in_dim(adapter_down_inputs, storage_block * TENANTS_PER_BLOCK, TENANTS_PER_BLOCK, 0)
        output_factor = lax.dynamic_slice_in_dim(adapter_down_outputs, storage_block * TENANTS_PER_BLOCK, TENANTS_PER_BLOCK, 0)
        rows = hidden[picked].astype(jnp.float32)
        part = jnp.einsum('us,ysc->uyc', rows, input_factor.astype(jnp.float32))
        ranks = jnp.sum(part * onehot[:, :, None], 1).astype(jnp.bfloat16)
        delta = jnp.dot(expand(onehot, ranks), output_factor.reshape(TENANTS_PER_BLOCK * ADAPTER_RANK, MODEL_WIDTH), preferred_element_type=jnp.float32).astype(jnp.bfloat16)
        total = total.at[picked].add(jnp.where(live[:, None], delta, jnp.zeros((), jnp.bfloat16)))
        return total, None

    delta_down, _ = lax.scan(down_step, jnp.zeros((TOKENS, MODEL_WIDTH), jnp.bfloat16), blocks)
    mixed = jnp.dot(hidden, down_matrix, preferred_element_type=jnp.float32) + delta_down.astype(jnp.float32)
    return mixed.astype(jnp.bfloat16)
```

```python
import jax
import jax.numpy as jnp
from jax import lax
from jax.sharding import Mesh, PartitionSpec as P

GRP = ("z", "c")
TP = ("x", "y")
BF = jnp.bfloat16
F32 = jnp.float32


def dot(a, b):
    return jnp.dot(a, b, preferred_element_type=F32)


def sum_over(values, axis):
    n = lax.axis_size(axis)
    many = jnp.broadcast_to(values[None], (n,) + values.shape)
    got = lax.all_to_all(many, axis, split_axis=0, concat_axis=0, tiled=True)
    return jnp.sum(got.astype(F32), 0)


def sum_tp(values):
    first = sum_over(values.astype(BF), "x").astype(BF)
    return sum_over(first, "y").astype(BF)


def spread_onehot(onehot, vec):
    wide = onehot[:, :, None] * vec[:, None, :]
    return wide.reshape(vec.shape[0], -1)


def body(
    tokens,
    token_tenant,
    tenant_storage_slot,
    gate_matrix,
    up_matrix,
    down_matrix,
    adapter_gate_up_inputs,
    adapter_gate_up_outputs,
    adapter_down_inputs,
    adapter_down_outputs,
):
    groups = lax.axis_size(GRP)
    shares = lax.axis_size(TP)
    rows = tokens.shape[0]
    block_slots = adapter_gate_up_inputs.shape[0]
    rank = adapter_gate_up_inputs.shape[2] // 2
    hidden_share = gate_matrix.shape[1]
    width_share = tokens.shape[1]
    capacity = 2 * rows // groups
    table = jnp.arange(tenant_storage_slot.shape[0], dtype=jnp.int32)
    match = token_tenant[:, None] == table[None, :]
    slot = jnp.sum(jnp.where(match, tenant_storage_slot[None, :], 0), 1)
    server = slot // block_slots
    local = slot - server * block_slots
    picks = (server[:, None] == jnp.arange(groups, dtype=jnp.int32)[None, :]).astype(jnp.int32)
    place = jnp.sum(picks * (jnp.cumsum(picks, 0) - 1), 1)
    position = server * capacity + place
    seats = jnp.arange(groups * capacity, dtype=jnp.int32)
    seat_of = (seats[:, None] == position[None, :]).astype(BF)
    row_of = (position[:, None] == seats[None, :]).astype(BF)

    def exchange(values):
        got = lax.all_to_all(
            values.reshape((groups, -1) + values.shape[1:]),
            GRP,
            split_axis=0,
            concat_axis=0,
            tiled=True,
        )
        return got

    def pack(values):
        return dot(seat_of, values).astype(BF)

    extra = 16
    taken = jnp.sum(
        jnp.where(seats[:, None] == position[None, :], local[None, :] + 1, 0), 1
    ).astype(BF)
    notes = jnp.pad(
        taken.reshape(groups, 1, capacity),
        ((0, 0), (0, extra - 1), (0, width_share - capacity)),
    )
    sent = jnp.concatenate([pack(tokens).reshape(groups, capacity, width_share), notes], 1)
    got = exchange(sent.reshape(groups * (capacity + extra), width_share))
    rows_flattened = got[:, :capacity].reshape(groups * capacity, width_share)
    owner = got[:, capacity, :capacity].reshape(-1).astype(F32)
    onehot = (owner[:, None] == jnp.arange(1, block_slots + 1, dtype=F32)[None, :]).astype(BF)
    onehot_wide = onehot.astype(F32)[:, :, None]
    part = jnp.einsum("ny,eyq->neq", rows_flattened, adapter_gate_up_inputs, preferred_element_type=F32)
    part = jnp.sum(part * onehot_wide, 1)
    ranks = sum_tp(part)
    gate_factor = adapter_gate_up_outputs[:, :rank, :].reshape(block_slots * rank, hidden_share)
    up_factor = adapter_gate_up_outputs[:, rank:, :].reshape(block_slots * rank, hidden_share)
    delta_gate = dot(spread_onehot(onehot, ranks[:, :rank]), gate_factor).astype(BF)
    delta_up = dot(spread_onehot(onehot, ranks[:, rank:]), up_factor).astype(BF)
    back_gate = exchange(delta_gate).reshape(groups * capacity, hidden_share)
    back_up = exchange(delta_up).reshape(groups * capacity, hidden_share)
    piece = lax.all_gather(tokens, TP, axis=1, tiled=True)
    gate = dot(piece, gate_matrix) + dot(row_of, back_gate)
    up = dot(piece, up_matrix) + dot(row_of, back_up)
    hidden = (jax.nn.silu(gate) * up).astype(BF)
    got_hidden = exchange(pack(hidden)).reshape(groups * capacity, hidden_share)
    down_part = jnp.einsum("us,ysc->uyc", got_hidden, adapter_down_inputs, preferred_element_type=F32)
    down_part = jnp.sum(down_part * onehot_wide, 1)
    down_ranks = sum_tp(down_part)
    down_factor = adapter_down_outputs.reshape(block_slots * rank, width_share)
    delta_down = dot(spread_onehot(onehot, down_ranks), down_factor).astype(BF)
    back_down = exchange(delta_down).reshape(groups * capacity, width_share)
    partial = dot(hidden, down_matrix).astype(BF)
    split = partial.reshape(rows, shares, width_share).transpose(1, 0, 2)
    parts = lax.all_to_all(split, TP, split_axis=0, concat_axis=0, tiled=True)
    result = jnp.sum(parts.astype(F32), 0) + dot(row_of, back_down)
    return result.astype(BF)


def solution(mesh):
    sizes = mesh.devices.shape
    cores = 2
    side = 4
    fine = Mesh(
        mesh.devices.reshape(sizes[0] // cores, cores, sizes[1] // side, side),
        ("z", "c", "x", "y"),
    )
    return jax.shard_map(
        body,
        mesh=fine,
        in_specs=(
            P(GRP, TP),
            P(GRP),
            P(),
            P(None, TP),
            P(None, TP),
            P(TP, None),
            P(GRP, TP, None),
            P(GRP, None, TP),
            P(GRP, TP, None),
            P(GRP, None, TP),
        ),
        out_specs=P(GRP, TP),
        check_vma=False,
    )
```

```python
import jax
import jax.numpy as jnp
from jax import lax
from jax.experimental import pallas as pl
from jax.experimental.pallas import tpu as pltpu
from jax.sharding import Mesh, PartitionSpec as P

GRP = ("z", "c")
TP = ("x", "y")
BF = jnp.bfloat16
F32 = jnp.float32


def dot(a, b):
    return jnp.dot(a, b, preferred_element_type=F32)


def sum_over(values, axis):
    n = lax.axis_size(axis)
    many = jnp.broadcast_to(values[None], (n,) + values.shape)
    got = lax.all_to_all(many, axis, split_axis=0, concat_axis=0, tiled=True)
    return jnp.sum(got.astype(F32), 0)


def sum_tp(values):
    first = sum_over(values.astype(BF), "x").astype(BF)
    return sum_over(first, "y").astype(BF)


def spread_onehot(onehot, vec):
    wide = onehot[:, :, None] * vec[:, None, :]
    return wide.reshape(vec.shape[0], -1)


def shift(values, axis, step):
    n = lax.axis_size(axis)
    return lax.ppermute(values, axis, [(i, (i + step) % n) for i in range(n)])


def swap(values):
    return shift(values, "c", 1)


def ring(values):
    half = values.shape[0] // 2
    below = shift(values, "z", 1)
    above = shift(values, "z", -1)
    low = shift(below[:half], "z", 1)
    high = shift(above[half:], "z", -1)
    return [values, below, above, jnp.concatenate([low, high], 0)]


def ring_order(server):
    z = lax.axis_index("z")
    c = lax.axis_index("c")
    n = lax.axis_size("z")
    apart = lax.rem(server // 2 - z + n, n)
    place = jnp.where(apart == 0, 0, jnp.where(apart == n - 1, 1, jnp.where(apart == 1, 2, 3)))
    return place + n * (lax.rem(server, 2) != c).astype(jnp.int32)


def peers(values, axis):
    return [values, shift(values, axis, 1), shift(values, axis, -1), shift(values, axis, 2)]


def peer_order(axis, which):
    step = jnp.where(which == 0, 0, jnp.where(which == 1, -1, jnp.where(which == 2, 1, 2)))
    n = lax.axis_size(axis)
    return lax.rem(lax.axis_index(axis) + step + n, n)


def base_kernel(order, a_ref, b_ref, gate_ref, up_ref, gate_out, up_out):
    half = a_ref.shape[2]
    a = a_ref[0, 0]
    b = b_ref[0, 0]
    first = pl.program_id(0) == 0
    for w_ref, out in ((gate_ref, gate_out), (up_ref, up_out)):
        w = w_ref[...]
        low = jnp.dot(a, w, preferred_element_type=F32)
        high = jnp.dot(b, w, preferred_element_type=F32)

        @pl.when(first)
        def _():
            out[:half] = low
            out[half:] = high

        @pl.when(jnp.logical_not(first))
        def _():
            out[:half] += low
            out[half:] += high


def base_products(tokens, gate_matrix, up_matrix):
    rows, share = tokens.shape
    half = rows // 2
    width = gate_matrix.shape[1]
    n = lax.axis_size("x")
    a_line = jnp.stack(peers(tokens[:half], "x"))
    b_line = jnp.stack(peers(tokens[half:], "y"))
    a_all = jnp.stack(peers(a_line, "y"))
    b_all = jnp.stack(peers(b_line, "x"))
    steps = jnp.arange(n * n, dtype=jnp.int32)
    order = peer_order("x", steps // n) * n + peer_order("y", lax.rem(steps, n))
    weight = pl.BlockSpec((share, width), lambda k, o: (o[k], 0))
    grid_spec = pltpu.PrefetchScalarGridSpec(
        num_scalar_prefetch=1,
        grid=(n * n,),
        in_specs=[
            pl.BlockSpec((1, 1, half, share), lambda k, o: (lax.rem(k, n), k // n, 0, 0)),
            pl.BlockSpec((1, 1, half, share), lambda k, o: (k // n, lax.rem(k, n), 0, 0)),
            weight,
            weight,
        ],
        out_specs=[pl.BlockSpec((rows, width), lambda k, o: (0, 0))] * 2,
    )
    return pl.pallas_call(
        base_kernel,
        grid_spec=grid_spec,
        out_shape=[jax.ShapeDtypeStruct((rows, width), F32)] * 2,
        name="base",
        cost_estimate=pl.CostEstimate(
            flops=4 * rows * share * n * n * width,
            bytes_accessed=4 * share * n * n * width + 12 * rows * width,
            transcendentals=0,
        ),
    )(order, a_all, b_all, gate_matrix, up_matrix)


def layer(
    tokens,
    token_tenant,
    tenant_storage_slot,
    gate_matrix,
    up_matrix,
    down_matrix,
    adapter_gate_up_inputs,
    adapter_gate_up_outputs,
    adapter_down_inputs,
    adapter_down_outputs,
):
    groups = lax.axis_size(GRP)
    shares = lax.axis_size(TP)
    rows = tokens.shape[0]
    block_slots = adapter_gate_up_inputs.shape[0]
    rank = adapter_gate_up_inputs.shape[2] // 2
    hidden_share = gate_matrix.shape[1]
    width_share = tokens.shape[1]
    capacity = 2 * rows // groups
    spread = block_slots * rank
    side = groups * capacity // 2

    out_factors = ring(adapter_gate_up_outputs)
    both = jnp.concatenate([adapter_down_inputs.swapaxes(1, 2), adapter_down_outputs], 2)
    both = both + out_factors[3][0, 0, 0] * 0
    down_factors = ring(both)
    base_gate, base_up = base_products(tokens, gate_matrix, up_matrix)

    table = jnp.arange(tenant_storage_slot.shape[0], dtype=jnp.int32)
    match = token_tenant[:, None] == table[None, :]
    slot = jnp.sum(jnp.where(match, tenant_storage_slot[None, :], 0), 1)
    server = slot // block_slots
    local = slot - server * block_slots
    picks = (server[:, None] == jnp.arange(groups, dtype=jnp.int32)[None, :]).astype(jnp.int32)
    place = jnp.sum(picks * (jnp.cumsum(picks, 0) - 1), 1)
    position = server * capacity + place
    near = ring_order(server) * capacity + place
    seats = jnp.arange(groups * capacity, dtype=jnp.int32)
    seat_of = (seats[:, None] == position[None, :]).astype(BF)
    row_of = (position[:, None] == seats[None, :]).astype(BF)
    near_seat_of = (seats[:, None] == near[None, :]).astype(BF)
    near_row_of = (near[:, None] == seats[None, :]).astype(BF)

    def exchange(values):
        return lax.all_to_all(
            values.reshape((groups, -1) + values.shape[1:]),
            GRP,
            split_axis=0,
            concat_axis=0,
            tiled=True,
        )

    extra = 16
    taken = jnp.sum(
        jnp.where(seats[:, None] == position[None, :], local[None, :] + 1, 0), 1
    ).astype(BF)
    notes = jnp.pad(
        taken.reshape(groups, 1, capacity),
        ((0, 0), (0, extra - 1), (0, width_share - capacity)),
    )
    packed = dot(seat_of, tokens).astype(BF).reshape(groups, capacity, width_share)
    sent = jnp.concatenate([packed, notes], 1)
    got = exchange(sent.reshape(groups * (capacity + extra), width_share))
    rows_flattened = got[:, :capacity].reshape(groups * capacity, width_share)
    owner = got[:, capacity, :capacity].reshape(-1).astype(F32)
    onehot = (owner[:, None] == jnp.arange(1, block_slots + 1, dtype=F32)[None, :]).astype(F32)
    part = jnp.einsum("ny,eyq->neq", rows_flattened, adapter_gate_up_inputs, preferred_element_type=F32)
    part = jnp.sum(part * onehot[:, :, None], 1).astype(BF)
    home_part = dot(row_of, exchange(part).reshape(groups * capacity, 2 * rank))
    ranks = sum_tp(home_part)

    lanes = jnp.arange(block_slots, dtype=jnp.int32)
    choice = (local[:, None] == lanes[None, :]).astype(BF)
    near_choice = dot(near_seat_of, choice).astype(BF)
    choices = jnp.concatenate([near_choice[:side], swap(near_choice[side:])], 0)
    near_ranks = dot(near_seat_of, ranks).astype(BF)
    all_ranks = jnp.concatenate([near_ranks[:side], swap(near_ranks[side:])], 0)

    def blocks_of(values):
        mine = values[:side].reshape((groups // 2, capacity) + values.shape[1:])
        other = values[side:].reshape((groups // 2, capacity) + values.shape[1:])
        both = jnp.concatenate([mine, other], 1)
        return [both[i] for i in range(groups // 2)]

    def home(outs):
        mine = jnp.concatenate([o[:capacity] for o in outs], 0)
        other = swap(jnp.concatenate([o[capacity:] for o in outs], 0))
        return mine, other

    def to_rows(halves):
        mine, other = halves
        return dot(near_row_of[:, :side], mine) + dot(near_row_of[:, side:], other)

    wide_gate = blocks_of(spread_onehot(choices, all_ranks[:, :rank]))
    wide_up = blocks_of(spread_onehot(choices, all_ranks[:, rank:]))
    delta_gate, delta_up = [], []
    for wg, wu, f in zip(wide_gate, wide_up, out_factors):
        delta_gate.append(dot(wg, f[:, :rank, :].reshape(spread, hidden_share)).astype(BF))
        delta_up.append(dot(wu, f[:, rank:, :].reshape(spread, hidden_share)).astype(BF))
    delta_gate = home(delta_gate)
    delta_up = home(delta_up)
    gate = base_gate + to_rows(delta_gate)
    up = base_up + to_rows(delta_up)
    hidden = (jax.nn.silu(gate) * up).astype(BF)

    near_hidden = dot(near_seat_of, hidden).astype(BF)
    all_hidden = jnp.concatenate([near_hidden[:side], swap(near_hidden[side:])], 0)
    down_parts = []
    for mine, ch, f in zip(blocks_of(all_hidden), blocks_of(choices), down_factors):
        factor = f[:, :, :hidden_share].reshape(spread, hidden_share)
        part = lax.dot_general(mine, factor, (((1,), (1,)), ((), ())), preferred_element_type=F32)
        part = part.reshape(-1, block_slots, rank) * ch.astype(F32)[:, :, None]
        down_parts.append(jnp.sum(part, 1).astype(BF))
    down_rows = to_rows(home(down_parts))
    down_ranks = sum_tp(down_rows)
    near_down = dot(near_seat_of, down_ranks).astype(BF)
    all_down = jnp.concatenate([near_down[:side], swap(near_down[side:])], 0)
    delta_down = []
    for w, f in zip(blocks_of(spread_onehot(choices, all_down)), down_factors):
        factor = f[:, :, hidden_share:].reshape(spread, width_share)
        delta_down.append(dot(w, factor).astype(BF))
    returned = to_rows(home(delta_down))

    partial = dot(hidden, down_matrix).astype(BF)
    split = partial.reshape(rows, shares, width_share).transpose(1, 0, 2)
    parts = lax.all_to_all(split, TP, split_axis=0, concat_axis=0, tiled=True)
    result = jnp.sum(parts.astype(F32), 0) + returned
    return result.astype(BF)


def solution(mesh):
    sizes = mesh.devices.shape
    cores = 2
    side = 4
    fine = Mesh(
        mesh.devices.reshape(sizes[0] // cores, cores, sizes[1] // side, side),
        ("z", "c", "x", "y"),
    )
    return jax.shard_map(
        layer,
        mesh=fine,
        in_specs=(
            P(GRP, TP),
            P(GRP),
            P(),
            P(None, TP),
            P(None, TP),
            P(TP, None),
            P(GRP, TP, None),
            P(GRP, None, TP),
            P(GRP, TP, None),
            P(GRP, None, TP),
        ),
        out_specs=P(GRP, TP),
        check_vma=False,
    )
```

```python
import jax
import jax.numpy as jnp
from jax import lax
from jax.experimental import pallas as pl
from jax.experimental.pallas import tpu as pltpu
from jax.sharding import Mesh, PartitionSpec as P

GRP = ("z", "c")
TP = ("x", "y")
BF = jnp.bfloat16
F32 = jnp.float32


def dot(a, b):
    return jnp.dot(a, b, preferred_element_type=F32)


def dot_bf(a, b):
    return dot(a, b).astype(BF)


def shift(values, axis, step):
    n = lax.axis_size(axis)
    return lax.ppermute(values, axis, [(i, (i + step) % n) for i in range(n)])


def swap(values):
    return shift(values, "c", 1)


def peers(values, axis):
    return [values, shift(values, axis, 1), shift(values, axis, -1), shift(values, axis, 2)]


def peer_order(axis, which):
    step = jnp.where(which == 0, 0, jnp.where(which == 1, -1, jnp.where(which == 2, 1, 2)))
    n = lax.axis_size(axis)
    return lax.rem(lax.axis_index(axis) + step + n, n)


def sum_over(values, axis):
    got = [v.astype(F32) for v in peers(values, axis)]
    return ((got[0] + got[1]) + (got[2] + got[3])).astype(BF)


def sum_tp(values):
    first = sum_over(values, "x")
    return sum_over(first, "y")


def scatter_over(values, axis, dim):
    n = lax.axis_size(axis)
    size = values.shape[dim] // n
    i = lax.axis_index(axis)

    def part(step):
        start = lax.rem(i + step + n, n) * size
        return lax.dynamic_slice_in_dim(values, start, size, dim)

    total = part(0).astype(F32)
    for step in (2, 1, -1):
        total = total + shift(part(step), axis, step).astype(F32)
    return total


def ring(pieces):
    half = pieces[0].shape[0] // 2
    below = [shift(v, "z", 1) for v in pieces]
    above = [shift(v, "z", -1) for v in pieces]
    far = [
        jnp.concatenate([shift(b[:half], "z", 1), shift(a[half:], "z", -1)], 0)
        for b, a in zip(below, above)
    ]
    return [pieces, below, above, far]


def base_kernel(order, a_ref, b_ref, w_ref, out):
    half = a_ref.shape[2]
    w = w_ref[...]
    low = jnp.dot(a_ref[0, 0], w, preferred_element_type=F32)
    high = jnp.dot(b_ref[0, 0], w, preferred_element_type=F32)
    first = pl.program_id(0) == 0

    @pl.when(first)
    def _():
        out[:half] = low
        out[half:] = high

    @pl.when(jnp.logical_not(first))
    def _():
        out[:half] += low
        out[half:] += high


def base_products(tokens, gate_matrix, up_matrix):
    rows, share = tokens.shape
    half = rows // 2
    width = gate_matrix.shape[1]
    n = lax.axis_size("x")
    a_line = jnp.stack(peers(tokens[:half], "x"))
    b_line = jnp.stack(peers(tokens[half:], "y"))
    a_all = jnp.stack(peers(a_line, "y"))
    b_all = jnp.stack(peers(b_line, "x"))
    steps = jnp.arange(n * n, dtype=jnp.int32)
    order = peer_order("x", steps // n) * n + peer_order("y", lax.rem(steps, n))
    weight = pl.BlockSpec((share, width), lambda k, o: (o[k], 0))
    grid_spec = pltpu.PrefetchScalarGridSpec(
        num_scalar_prefetch=1,
        grid=(n * n,),
        in_specs=[
            pl.BlockSpec((1, 1, half, share), lambda k, o: (lax.rem(k, n), k // n, 0, 0)),
            pl.BlockSpec((1, 1, half, share), lambda k, o: (k // n, lax.rem(k, n), 0, 0)),
            weight,
        ],
        out_specs=pl.BlockSpec((rows, width), lambda k, o: (0, 0)),
    )

    def product(matrix):
        return pl.pallas_call(
            base_kernel,
            grid_spec=grid_spec,
            out_shape=jax.ShapeDtypeStruct((rows, width), F32),
            name="base",
            cost_estimate=pl.CostEstimate(
                flops=2 * rows * share * n * n * width,
                bytes_accessed=2 * share * n * n * width + 6 * rows * width,
                transcendentals=0,
            ),
        )(order, a_all, b_all, matrix)

    base_gate = product(gate_matrix)
    base_up = product(up_matrix)
    return base_gate, base_up


def layer(
    tokens,
    token_tenant,
    tenant_storage_slot,
    gate_matrix,
    up_matrix,
    down_matrix,
    adapter_gate_up_inputs,
    adapter_gate_up_outputs,
    adapter_down_inputs,
    adapter_down_outputs,
):
    groups = lax.axis_size(GRP)
    rows = tokens.shape[0]
    block_slots = adapter_gate_up_inputs.shape[0]
    rank = adapter_gate_up_inputs.shape[2] // 2
    hidden_share = gate_matrix.shape[1]
    width_share = tokens.shape[1]
    capacity = 2 * rows // groups
    chips = groups // 2
    spread = block_slots * rank
    side = chips * capacity

    in_factors = ring([adapter_gate_up_inputs])
    gate_part = adapter_gate_up_outputs[:, :rank, :]
    up_part = adapter_gate_up_outputs[:, rank:, :]
    out_factors = ring([gate_part, up_part])
    down_factors = ring([adapter_down_inputs.swapaxes(1, 2), adapter_down_outputs])
    base_gate, base_up = base_products(tokens, gate_matrix, up_matrix)

    tokens_pair = (tokens, swap(tokens))
    tenants = jnp.stack([token_tenant, swap(token_tenant)])
    table = jnp.arange(tenant_storage_slot.shape[0], dtype=jnp.int32)
    match = tenants[:, :, None] == table[None, None, :]
    slot = jnp.sum(jnp.where(match, tenant_storage_slot[None, None, :], 0), 2)
    server = slot // block_slots
    local = slot - server * block_slots
    picks = (server[:, :, None] == jnp.arange(groups, dtype=jnp.int32)).astype(jnp.int32)
    place = jnp.sum(picks * (jnp.cumsum(picks, 1) - 1), 2)
    apart = lax.rem(server // 2 - lax.axis_index("z") + chips, chips)
    turn = jnp.where(apart == 0, 0, jnp.where(apart == chips - 1, 1, jnp.where(apart == 1, 2, 3)))
    seat = turn * capacity + place
    mine = lax.rem(server, 2) == lax.axis_index("c")
    here = jnp.where(mine, seat, -1)
    there = jnp.where(mine, -1, seat)[0]
    seats = jnp.arange(side, dtype=jnp.int32)
    take = (seats[None, :, None] == here[:, None, :]).astype(BF)
    give_here = (here[0][:, None] == seats[None, :]).astype(BF)
    give_there = (there[:, None] == seats[None, :]).astype(BF)
    seat_local = jnp.sum(jnp.where(seats[None, :, None] == here[:, None, :], local[:, None, :], 0), 2)
    seat_local = seat_local.reshape(2, chips, capacity).transpose(1, 0, 2).reshape(chips, 2 * capacity)

    def by_block(pair):
        packed = [dot_bf(take[g], v).reshape(chips, capacity, -1) for g, v in enumerate(pair)]
        return jnp.concatenate(packed, 1)

    def home(outs):
        own = jnp.concatenate([o[:capacity] for o in outs], 0)
        other = swap(jnp.concatenate([o[capacity:] for o in outs], 0))
        return dot(give_here, own) + dot(give_there, other)

    def lane_mask(i, width):
        lane = jnp.arange(block_slots * width, dtype=jnp.int32) // width
        return seat_local[i][:, None] == lane[None, :]

    def fan(start, width):
        lane = lax.rem(jnp.arange(spread, dtype=jnp.int32), rank)
        return (jnp.arange(width, dtype=jnp.int32)[:, None] == lane[None, :] + start).astype(BF)

    def wide(i, packed, start):
        spread_out = dot(packed, fan(start, packed.shape[1]))
        return jnp.where(lane_mask(i, rank), spread_out, 0.0).astype(BF)

    seated = by_block(tokens_pair)
    parts = []
    for i, (f,) in enumerate(in_factors):
        part = jnp.einsum("ny,eyq->neq", seated[i], f, preferred_element_type=F32)
        chosen = seat_local[i][:, None] == jnp.arange(block_slots, dtype=jnp.int32)[None, :]
        parts.append(jnp.sum(part * chosen.astype(F32)[:, :, None], 1).astype(BF))
    home_part = home(parts).astype(BF)
    ranks = sum_tp(home_part)
    seated_ranks = by_block((ranks, swap(ranks)))

    delta_gate, delta_up = [], []
    for i, (g, u) in enumerate(out_factors):
        delta_gate.append(dot_bf(wide(i, seated_ranks[i], 0), g.reshape(spread, hidden_share)))
        delta_up.append(dot_bf(wide(i, seated_ranks[i], rank), u.reshape(spread, hidden_share)))
    gate = base_gate + home(delta_gate)
    up = base_up + home(delta_up)
    hidden = (jax.nn.silu(gate) * up).astype(BF)

    partial = dot_bf(hidden, down_matrix)
    half = rows // 2
    n = lax.axis_size("x")
    low = scatter_over(partial[:half], "x", 1).astype(BF)
    high = partial[half:].reshape(half, n, n, width_share)
    high = scatter_over(high, "y", 2).astype(BF)
    low = scatter_over(low, "y", 1)
    high = scatter_over(high.reshape(half, n, width_share), "x", 1).reshape(half, width_share)

    seated_hidden = by_block((hidden, swap(hidden)))
    down_parts = []
    for i, (d, _) in enumerate(down_factors):
        part = lax.dot_general(
            seated_hidden[i],
            d.reshape(spread, hidden_share),
            (((1,), (1,)), ((), ())),
            preferred_element_type=F32,
        )
        part = jnp.where(lane_mask(i, rank), part, 0.0).astype(BF)
        down_parts.append(dot_bf(part, fan(0, rank).T))
    down_rows = home(down_parts).astype(BF)
    down_ranks = sum_tp(down_rows)
    seated_down = by_block((down_ranks, swap(down_ranks)))
    delta_down = [
        dot_bf(wide(i, seated_down[i], 0), o.reshape(spread, width_share))
        for i, (_, o) in enumerate(down_factors)
    ]
    returned = home(delta_down)
    return (jnp.concatenate([low, high], 0) + returned).astype(BF)


def solution(mesh):
    sizes = mesh.devices.shape
    cores = 2
    side = 4
    fine = Mesh(
        mesh.devices.reshape(sizes[0] // cores, cores, sizes[1] // side, side),
        ("z", "c", "x", "y"),
    )
    return jax.shard_map(
        layer,
        mesh=fine,
        in_specs=(
            P(GRP, TP),
            P(GRP),
            P(),
            P(None, TP),
            P(None, TP),
            P(TP, None),
            P(GRP, TP, None),
            P(GRP, None, TP),
            P(GRP, TP, None),
            P(GRP, None, TP),
        ),
        out_specs=P(GRP, TP),
        check_vma=False,
    )
```

```python
import functools

import jax
import jax.numpy as jnp
from jax import lax
from jax.experimental import pallas as pl
from jax.experimental.pallas import tpu as pltpu
from jax.sharding import Mesh, PartitionSpec as P

GRP = ("z", "c")
TP = ("x", "y")
BF = jnp.bfloat16
F32 = jnp.float32
FAN = 4


def dot(a, b):
    return jnp.dot(a, b, preferred_element_type=F32)


def dot_bf(a, b):
    return dot(a, b).astype(BF)


def shift(values, axis, step):
    n = lax.axis_size(axis)
    return lax.ppermute(values, axis, [(i, (i + step) % n) for i in range(n)])


def swap(values):
    return shift(values, "c", 1)


def over_tp(values):
    return lax.all_to_all(values, TP, split_axis=0, concat_axis=0, tiled=True)


def sum_over(values, axis):
    got = [shift(values, axis, step).astype(F32) for step in (1, -1, 2)]
    return ((values.astype(F32) + got[0]) + (got[1] + got[2])).astype(BF)


def sum_tp_steps(values):
    first = sum_over(values, "x")
    return sum_over(first, "y")


def sum_tp_parts(values):
    shares = lax.axis_size(TP)
    rows, width = values.shape
    got = over_tp(values.reshape(shares, rows // shares, width))
    own = jnp.sum(got.astype(F32), 0).astype(BF)
    return over_tp(jnp.broadcast_to(own[None], (shares,) + own.shape)).reshape(rows, width)


def ring(first, second):
    below = (shift(first, "z", 1), shift(second, "z", 1))
    above = (shift(first, "z", -1), shift(second, "z", -1))
    far = (shift(below[0], "z", 1), shift(above[1], "z", -1))
    return [(first, second), below, above, far]


def base_kernel(tokens_ref, w_ref, out_ref):
    tokens = jnp.concatenate([tokens_ref[i] for i in range(tokens_ref.shape[0])], 1)
    product = dot(tokens, w_ref[...])
    first = pl.program_id(0) == 0

    @pl.when(first)
    def _():
        out_ref[...] = product

    @pl.when(jnp.logical_not(first))
    def _():
        out_ref[...] += product


def base_product(pieces, matrix):
    shares, rows, share = pieces.shape
    width = matrix.shape[1]
    return pl.pallas_call(
        base_kernel,
        grid=(shares // FAN,),
        in_specs=[
            pl.BlockSpec((FAN, rows, share), lambda k: (k, 0, 0)),
            pl.BlockSpec((FAN * share, width), lambda k: (k, 0)),
        ],
        out_specs=pl.BlockSpec((rows, width), lambda k: (0, 0)),
        out_shape=jax.ShapeDtypeStruct((rows, width), F32),
        name="base",
        cost_estimate=pl.CostEstimate(
            flops=2 * rows * share * shares * width,
            bytes_accessed=2 * share * shares * width + 6 * rows * width,
            transcendentals=0,
        ),
    )(pieces, matrix)


def down_kernel(hidden_ref, w_ref, out_ref):
    product = dot_bf(hidden_ref[...], w_ref[...])
    share = out_ref.shape[2]
    for i in range(out_ref.shape[0]):
        out_ref[i] = product[:, i * share : (i + 1) * share]


def down_product(hidden, matrix, shares):
    rows, depth = hidden.shape
    share = matrix.shape[1] // shares
    return pl.pallas_call(
        down_kernel,
        grid=(shares // FAN,),
        in_specs=[
            pl.BlockSpec((rows, depth), lambda k: (0, 0)),
            pl.BlockSpec((depth, FAN * share), lambda k: (0, k)),
        ],
        out_specs=pl.BlockSpec((FAN, rows, share), lambda k: (k, 0, 0)),
        out_shape=jax.ShapeDtypeStruct((shares, rows, share), BF),
        name="partial",
        cost_estimate=pl.CostEstimate(
            flops=2 * rows * depth * share * shares,
            bytes_accessed=2 * (depth + rows) * share * shares + 2 * rows * depth,
            transcendentals=0,
        ),
    )(hidden, matrix)


def fan_out(start, depth, rank, slots):
    lane = lax.broadcasted_iota(jnp.int32, (depth, slots * rank), 1)
    row = lax.broadcasted_iota(jnp.int32, (depth, slots * rank), 0)
    return (row == lax.rem(lane, rank) + start).astype(BF)


def slot_mask(local, rows, rank, first, slots):
    lane = lax.broadcasted_iota(jnp.int32, (rows, slots * rank), 1) // rank + first
    return local.astype(F32).astype(jnp.int32) == lane


def split_rows(values, own_ref, other_ref, i):
    half = values.shape[0] // 2
    rows = pl.ds(i * half, half)
    return (own_ref, rows, values[:half]), (other_ref, rows, values[half:])


def delta_kernel(count, rank, *refs):
    ranks_ref, local_ref = refs[:2]
    factors = refs[2 : 2 + 2 * count]
    own_ref, other_ref = refs[2 + 2 * count :]
    slots = factors[0].shape[0]
    width = factors[0].shape[2]
    rows = ranks_ref.shape[1]
    for which in range(2):
        fan = fan_out(which * rank, ranks_ref.shape[2], rank, slots)
        for i in range(count):
            wide = dot(ranks_ref[i], fan)
            wide = jnp.where(slot_mask(local_ref[i], rows, rank, 0, slots), wide, 0.0).astype(BF)
            delta = dot_bf(wide, factors[2 * i + which][...].reshape(slots * rank, width))
            for ref, at, part in split_rows(delta, own_ref, other_ref, i):
                ref[at, which * width : (which + 1) * width] = part


def down_rank_kernel(count, rank, *refs):
    hidden_ref, local_ref = refs[:2]
    factors = refs[2 : 2 + 2 * count]
    own_ref, other_ref = refs[2 + 2 * count :]
    slots = factors[0].shape[0]
    rows, depth = hidden_ref.shape[1:]
    fan = fan_out(0, rank, rank, slots)
    for i in range(count):
        total = jnp.zeros((rows, rank), F32)
        for which in range(2):
            factor = factors[2 * i + which][:, :, :depth].reshape(slots * rank, depth)
            part = lax.dot_general(
                hidden_ref[i], factor, (((1,), (1,)), ((), ())), preferred_element_type=F32
            )
            mask = slot_mask(local_ref[i], rows, rank, which * slots, slots)
            part = jnp.where(mask, part, 0.0).astype(BF)
            total += lax.dot_general(part, fan, (((1,), (1,)), ((), ())), preferred_element_type=F32)
        for ref, at, part in split_rows(total.astype(BF), own_ref, other_ref, i):
            ref[at, :] = part


def down_delta_kernel(count, rank, *refs):
    ranks_ref, local_ref = refs[:2]
    factors = refs[2 : 2 + 2 * count]
    own_ref, other_ref = refs[2 + 2 * count :]
    slots = factors[0].shape[0]
    rows = ranks_ref.shape[1]
    width = own_ref.shape[1]
    fan = fan_out(0, rank, rank, slots)
    for i in range(count):
        total = jnp.zeros((rows, width), F32)
        spread = dot(ranks_ref[i], fan)
        for which in range(2):
            mask = slot_mask(local_ref[i], rows, rank, which * slots, slots)
            wide = jnp.where(mask, spread, 0.0).astype(BF)
            factor = factors[2 * i + which]
            factor = factor[:, :, factor.shape[2] - width :].reshape(slots * rank, width)
            total += dot(wide, factor)
        for ref, at, part in split_rows(total.astype(BF), own_ref, other_ref, i):
            ref[at, :] = part


def seated_call(kernel, rank, seated, local, factors, width, flops):
    count, rows = seated.shape[:2]
    out = jax.ShapeDtypeStruct((count * rows // 2, width), BF)
    flat = [f for pair in factors for f in pair]
    moved = sum(2 * f.size for f in flat) + 4 * out.size + 2 * seated.size
    return pl.pallas_call(
        functools.partial(kernel, count, rank),
        in_specs=[pl.BlockSpec(memory_space=pltpu.VMEM)] * (2 + len(flat)),
        out_specs=[pl.BlockSpec(memory_space=pltpu.VMEM)] * 2,
        out_shape=[out, out],
        cost_estimate=pl.CostEstimate(flops=flops, bytes_accessed=moved, transcendentals=0),
    )(seated, local, *flat)


def layer(
    tokens,
    token_tenant,
    tenant_storage_slot,
    gate_matrix,
    up_matrix,
    down_matrix,
    adapter_gate_up_inputs,
    adapter_gate_up_outputs,
    adapter_down_inputs,
    adapter_down_outputs,
):
    groups = lax.axis_size(GRP)
    shares = lax.axis_size(TP)
    rows = tokens.shape[0]
    block_slots = adapter_gate_up_inputs.shape[0]
    rank = adapter_gate_up_inputs.shape[2] // 2
    hidden_share = gate_matrix.shape[1]
    width_share = tokens.shape[1]
    capacity = 2 * rows // groups
    chips = groups // 2
    side = chips * capacity
    near = (chips - 1) * capacity

    in_factors = [adapter_gate_up_inputs]
    in_factors += [shift(adapter_gate_up_inputs, "z", step) for step in (1, -1, 2)]
    pieces = over_tp(jnp.broadcast_to(tokens[None], (shares,) + tokens.shape))
    gate_part = adapter_gate_up_outputs[:, :rank, :]
    up_part = adapter_gate_up_outputs[:, rank:, :]
    out_factors = ring(gate_part, up_part)
    down_in = adapter_down_inputs.swapaxes(1, 2)
    half = block_slots // 2
    low = jnp.concatenate([down_in[:half], adapter_down_outputs[:half]], 2)
    high = jnp.concatenate([down_in[half:], adapter_down_outputs[half:]], 2)
    down_factors = ring(low, high)
    base_gate = base_product(pieces, gate_matrix)
    base_up = base_product(pieces, up_matrix)

    tokens_pair = (tokens, swap(tokens))
    tenants = jnp.stack([token_tenant, swap(token_tenant)])
    table = jnp.arange(tenant_storage_slot.shape[0], dtype=jnp.int32)
    match = tenants[:, :, None] == table[None, None, :]
    slot = jnp.sum(jnp.where(match, tenant_storage_slot[None, None, :], 0), 2)
    server = slot // block_slots
    local = slot - server * block_slots
    picks = (server[:, :, None] == jnp.arange(groups, dtype=jnp.int32)).astype(jnp.int32)
    place = jnp.sum(picks * (jnp.cumsum(picks, 1) - 1), 2)
    apart = lax.rem(server // 2 - lax.axis_index("z") + chips, chips)
    turn = jnp.where(apart == 0, 0, jnp.where(apart == chips - 1, 1, jnp.where(apart == 1, 2, 3)))
    seat = turn * capacity + place
    mine = lax.rem(server, 2) == lax.axis_index("c")
    here = jnp.where(mine, seat, -1)
    there = jnp.where(mine, -1, seat)[0]
    seats = jnp.arange(side, dtype=jnp.int32)
    take = (seats[None, :, None] == here[:, None, :]).astype(BF)
    give_here = (here[0][:, None] == seats[None, :]).astype(BF)
    give_there = (there[:, None] == seats[None, :]).astype(BF)

    def by_block(pair):
        packed = [dot_bf(take[g], v).reshape(chips, capacity, -1) for g, v in enumerate(pair)]
        return jnp.concatenate(packed, 1)

    def home(own, other, start):
        stop = start + own.shape[0]
        return dot(give_here[:, start:stop], own) + dot(give_there[:, start:stop], other)

    seat_local = by_block((local[0][:, None].astype(BF), local[1][:, None].astype(BF)))

    seated = by_block(tokens_pair)
    chosen = seat_local.astype(F32) == jnp.arange(block_slots, dtype=F32)[None, None, :]
    parts = []
    for i, f in enumerate(in_factors):
        part = jnp.einsum("ny,eyq->neq", seated[i], f, preferred_element_type=F32)
        parts.append(jnp.sum(part * chosen[i].astype(F32)[:, :, None], 1).astype(BF))
    own = jnp.concatenate([o[:capacity] for o in parts], 0)
    other = swap(jnp.concatenate([o[capacity:] for o in parts], 0))
    home_part = home(own, other, 0).astype(BF)
    ranks = sum_tp_parts(home_part)
    seated_ranks = by_block((ranks, swap(ranks)))

    def deltas(first, last):
        count = last - first
        flops = 4 * 2 * capacity * count * block_slots * rank * hidden_share
        return seated_call(
            delta_kernel,
            rank,
            seated_ranks[first:last],
            seat_local[first:last],
            out_factors[first:last],
            2 * hidden_share,
            flops,
        )

    own, other = deltas(0, chips - 1)
    other = swap(other)
    gate = base_gate + home(own[:, :hidden_share], other[:, :hidden_share], 0)
    up = base_up + home(own[:, hidden_share:], other[:, hidden_share:], 0)
    own, other = deltas(chips - 1, chips)
    other = swap(other)
    gate = gate + home(own[:, :hidden_share], other[:, :hidden_share], near)
    up = up + home(own[:, hidden_share:], other[:, hidden_share:], near)
    hidden = (jax.nn.silu(gate) * up).astype(BF)

    partial = down_product(hidden, down_matrix, shares)
    hidden_pair = (hidden, swap(hidden))
    summed = over_tp(partial)

    seated_hidden = by_block(hidden_pair)
    flops = 4 * side * block_slots * rank * hidden_share
    own, other = seated_call(
        down_rank_kernel, rank, seated_hidden, seat_local, down_factors, rank, flops
    )
    down_rows = home(own, swap(other), 0).astype(BF)
    down_ranks = sum_tp_steps(down_rows)
    seated_down = by_block((down_ranks, swap(down_ranks)))
    flops = 4 * side * block_slots * rank * width_share
    own, other = seated_call(
        down_delta_kernel, rank, seated_down, seat_local, down_factors, width_share, flops
    )
    returned = home(own, swap(other), 0)
    return (jnp.sum(summed.astype(F32), 0) + returned).astype(BF)


def solution(mesh):
    sizes = mesh.devices.shape
    cores = 2
    side = 4
    fine = Mesh(
        mesh.devices.reshape(sizes[0] // cores, cores, sizes[1] // side, side),
        ("z", "c", "x", "y"),
    )
    return jax.shard_map(
        layer,
        mesh=fine,
        in_specs=(
            P(GRP, TP),
            P(GRP),
            P(),
            P(None, TP),
            P(None, TP),
            P(TP, None),
            P(GRP, TP, None),
            P(GRP, None, TP),
            P(GRP, TP, None),
            P(GRP, None, TP),
        ),
        out_specs=P(GRP, TP),
        check_vma=False,
    )
```

```python
import functools

import jax
import jax.numpy as jnp
from jax import lax
from jax.experimental import pallas as pl
from jax.experimental.pallas import tpu as pltpu
from jax.sharding import Mesh, PartitionSpec as P

GRP = ("z", "c")
TP = ("x", "y")
BF = jnp.bfloat16
F32 = jnp.float32


def dot(a, b):
    return jnp.dot(a, b, preferred_element_type=F32)


def dot_bf(a, b):
    return dot(a, b).astype(BF)


def shift(values, axis, step):
    n = lax.axis_size(axis)
    return lax.ppermute(values, axis, [(i, (i + step) % n) for i in range(n)])


def swap(values):
    return shift(values, "c", 1)


def sum_over(values, axis):
    got = [shift(values, axis, step).astype(F32) for step in (1, -1, 2)]
    return ((values.astype(F32) + got[0]) + (got[1] + got[2])).astype(BF)


def sum_tp(values):
    first = sum_over(values, "x")
    return sum_over(first, "y")


def ring(first, second):
    below = (shift(first, "z", 1), shift(second, "z", 1))
    above = (shift(first, "z", -1), shift(second, "z", -1))
    far = (shift(below[0], "z", 1), shift(above[1], "z", -1))
    return [(first, second), below, above, far]


def base_kernel(order, a_ref, b_ref, wa_ref, wb_ref, out_ref):
    n, _, part = a_ref.shape[1:]
    pieces = [a_ref[0, order[2 * n + i]] for i in range(n)]
    pieces += [b_ref[0, order[3 * n + i]] for i in range(n)]
    width = wa_ref.shape[-1]
    wa = wa_ref[...].reshape(n * part, width)
    wb = wb_ref[...].reshape(n * part, width)
    product = dot(jnp.concatenate(pieces, 1), jnp.concatenate([wa, wb], 0))
    first = pl.program_id(0) == 0

    @pl.when(first)
    def _():
        out_ref[...] = product

    @pl.when(jnp.logical_not(first))
    def _():
        out_ref[...] += product


def peers(values, axis):
    return jnp.stack([values] + [shift(values, axis, step) for step in (1, -1, 2)])


def index_order(axis, sign):
    n = lax.axis_size(axis)
    which = jnp.arange(n, dtype=jnp.int32)
    step = jnp.where(which == 0, 0, jnp.where(which == 1, 1, jnp.where(which == 2, -1, 2)))
    return lax.rem(lax.axis_index(axis) + sign * step + n, n).astype(jnp.int32)


def place_order(axis):
    n = lax.axis_size(axis)
    apart = lax.rem(lax.axis_index(axis) - jnp.arange(n, dtype=jnp.int32) + n, n)
    return jnp.where(apart == 0, 0, jnp.where(apart == 1, 1, jnp.where(apart == n - 1, 2, 3)))


def gather_tokens(tokens):
    part = tokens.shape[1] // 2
    a_line = peers(tokens[:, :part], "x")
    b_line = peers(tokens[:, part:], "y")
    return peers(a_line, "y"), peers(b_line, "x")


def base_product(pieces, matrix):
    a_all, b_all = pieces
    n, _, rows, part = a_all.shape
    width = matrix.shape[1]
    order = jnp.concatenate(
        [index_order("y", -1), index_order("x", -1), place_order("x"), place_order("y")]
    )
    weights = matrix.reshape(n, n, 2, part, width)
    line = pl.BlockSpec((1, n, rows, part), lambda k, o: (k, 0, 0, 0))
    grid_spec = pltpu.PrefetchScalarGridSpec(
        num_scalar_prefetch=1,
        grid=(n,),
        in_specs=[
            line,
            line,
            pl.BlockSpec((n, 1, 1, part, width), lambda k, o: (0, o[k], 0, 0, 0)),
            pl.BlockSpec((1, n, 1, part, width), lambda k, o: (o[n + k], 0, 1, 0, 0)),
        ],
        out_specs=pl.BlockSpec((rows, width), lambda k, o: (0, 0)),
    )
    return pl.pallas_call(
        base_kernel,
        grid_spec=grid_spec,
        out_shape=jax.ShapeDtypeStruct((rows, width), F32),
        name="base",
        cost_estimate=pl.CostEstimate(
            flops=2 * rows * matrix.size,
            bytes_accessed=2 * matrix.size + 2 * a_all.size + 2 * b_all.size + 4 * rows * width,
            transcendentals=0,
        ),
    )(order, a_all, b_all, weights, weights)


def down_kernel(order, hidden_ref, w_ref, *outs):
    n = len(outs) // 2
    half, span = outs[0].shape
    share = span // n
    step = pl.program_id(0)
    for m in range(n):
        start = pl.multiple_of(order[n + m] * share, share)
        product = dot_bf(hidden_ref[...], w_ref[:, pl.ds(start, share)])
        outs[n + m][:, pl.ds(pl.multiple_of(step * share, share), share)] = product[half:]
        for k in range(n):

            @pl.when(step == k)
            def _(k=k, m=m, product=product):
                outs[k][:, m * share : (m + 1) * share] = product[:half]


def down_product(hidden, matrix, n):
    rows, depth = hidden.shape
    span = matrix.shape[1] // n
    order = jnp.concatenate([index_order("x", 1), index_order("y", 1)])
    grid_spec = pltpu.PrefetchScalarGridSpec(
        num_scalar_prefetch=1,
        grid=(n,),
        in_specs=[
            pl.BlockSpec((rows, depth), lambda k, o: (0, 0)),
            pl.BlockSpec((depth, span), lambda k, o: (0, o[k])),
        ],
        out_specs=[pl.BlockSpec((rows // 2, span), lambda k, o: (0, 0))] * (2 * n),
    )
    outs = pl.pallas_call(
        down_kernel,
        grid_spec=grid_spec,
        out_shape=[jax.ShapeDtypeStruct((rows // 2, span), BF)] * (2 * n),
        name="partial",
        cost_estimate=pl.CostEstimate(
            flops=2 * rows * matrix.size,
            bytes_accessed=2 * matrix.size + 2 * hidden.size + 2 * rows * matrix.shape[1],
            transcendentals=0,
        ),
    )(order, hidden, matrix)
    return outs[:n], outs[n:]


def scatter_over(parts, axis):
    got = [shift(part, axis, step).astype(F32) for part, step in zip(parts[1:], (1, -1, 2))]
    return (parts[0].astype(F32) + got[0]) + (got[1] + got[2])


def scatter_sum(parts):
    low, high = parts
    n = len(low)
    low = scatter_over(low, "x").astype(BF)
    high = scatter_over(high, "y").astype(BF)
    low = scatter_over(jnp.split(low, n, 1), "y")
    high = scatter_over(jnp.split(high, n, 1), "x")
    return jnp.concatenate([low, high], 0)


def fan_out(start, depth, rank, slots):
    lane = lax.broadcasted_iota(jnp.int32, (depth, slots * rank), 1)
    row = lax.broadcasted_iota(jnp.int32, (depth, slots * rank), 0)
    return (row == lax.rem(lane, rank) + start).astype(BF)


def slot_mask(local, rows, rank, first, slots):
    lane = lax.broadcasted_iota(jnp.int32, (rows, slots * rank), 1) // rank + first
    return local.astype(F32).astype(jnp.int32) == lane


def split_rows(values, own_ref, other_ref, i):
    half = values.shape[0] // 2
    rows = pl.ds(i * half, half)
    return (own_ref, rows, values[:half]), (other_ref, rows, values[half:])


def delta_kernel(count, rank, *refs):
    ranks_ref, local_ref = refs[:2]
    factors = refs[2 : 2 + 2 * count]
    own_ref, other_ref = refs[2 + 2 * count :]
    slots = factors[0].shape[0]
    width = factors[0].shape[2]
    rows = ranks_ref.shape[1]
    for which in range(2):
        fan = fan_out(which * rank, ranks_ref.shape[2], rank, slots)
        for i in range(count):
            wide = dot(ranks_ref[i], fan)
            wide = jnp.where(slot_mask(local_ref[i], rows, rank, 0, slots), wide, 0.0).astype(BF)
            delta = dot_bf(wide, factors[2 * i + which][...].reshape(slots * rank, width))
            for ref, at, part in split_rows(delta, own_ref, other_ref, i):
                ref[at, which * width : (which + 1) * width] = part


def down_rank_kernel(count, rank, *refs):
    hidden_ref, local_ref = refs[:2]
    factors = refs[2 : 2 + 2 * count]
    own_ref, other_ref = refs[2 + 2 * count :]
    slots = factors[0].shape[0]
    rows, depth = hidden_ref.shape[1:]
    fan = fan_out(0, rank, rank, slots)
    for i in range(count):
        total = jnp.zeros((rows, rank), F32)
        for which in range(2):
            factor = factors[2 * i + which][:, :, :depth].reshape(slots * rank, depth)
            part = lax.dot_general(
                hidden_ref[i], factor, (((1,), (1,)), ((), ())), preferred_element_type=F32
            )
            mask = slot_mask(local_ref[i], rows, rank, which * slots, slots)
            part = jnp.where(mask, part, 0.0).astype(BF)
            total += lax.dot_general(part, fan, (((1,), (1,)), ((), ())), preferred_element_type=F32)
        for ref, at, part in split_rows(total.astype(BF), own_ref, other_ref, i):
            ref[at, :] = part


def down_delta_kernel(count, rank, *refs):
    ranks_ref, local_ref = refs[:2]
    factors = refs[2 : 2 + 2 * count]
    own_ref, other_ref = refs[2 + 2 * count :]
    slots = factors[0].shape[0]
    rows = ranks_ref.shape[1]
    width = own_ref.shape[1]
    fan = fan_out(0, rank, rank, slots)
    for i in range(count):
        total = jnp.zeros((rows, width), F32)
        spread = dot(ranks_ref[i], fan)
        for which in range(2):
            mask = slot_mask(local_ref[i], rows, rank, which * slots, slots)
            wide = jnp.where(mask, spread, 0.0).astype(BF)
            factor = factors[2 * i + which]
            factor = factor[:, :, factor.shape[2] - width :].reshape(slots * rank, width)
            total += dot(wide, factor)
        for ref, at, part in split_rows(total.astype(BF), own_ref, other_ref, i):
            ref[at, :] = part


def seated_call(kernel, rank, seated, local, factors, width, flops):
    count, rows = seated.shape[:2]
    out = jax.ShapeDtypeStruct((count * rows // 2, width), BF)
    flat = [f for pair in factors for f in pair]
    moved = sum(2 * f.size for f in flat) + 4 * out.size + 2 * seated.size
    return pl.pallas_call(
        functools.partial(kernel, count, rank),
        in_specs=[pl.BlockSpec(memory_space=pltpu.VMEM)] * (2 + len(flat)),
        out_specs=[pl.BlockSpec(memory_space=pltpu.VMEM)] * 2,
        out_shape=[out, out],
        cost_estimate=pl.CostEstimate(flops=flops, bytes_accessed=moved, transcendentals=0),
    )(seated, local, *flat)


def layer(
    tokens,
    token_tenant,
    tenant_storage_slot,
    gate_matrix,
    up_matrix,
    down_matrix,
    adapter_gate_up_inputs,
    adapter_gate_up_outputs,
    adapter_down_inputs,
    adapter_down_outputs,
):
    groups = lax.axis_size(GRP)
    rows = tokens.shape[0]
    block_slots = adapter_gate_up_inputs.shape[0]
    rank = adapter_gate_up_inputs.shape[2] // 2
    hidden_share = gate_matrix.shape[1]
    width_share = tokens.shape[1]
    capacity = 2 * rows // groups
    chips = groups // 2
    side = chips * capacity
    near = (chips - 1) * capacity

    in_factors = [adapter_gate_up_inputs]
    in_factors += [shift(adapter_gate_up_inputs, "z", step) for step in (1, -1, 2)]
    pieces = gather_tokens(tokens)
    gate_part = adapter_gate_up_outputs[:, :rank, :]
    up_part = adapter_gate_up_outputs[:, rank:, :]
    out_factors = ring(gate_part, up_part)
    down_in = adapter_down_inputs.swapaxes(1, 2)
    half = block_slots // 2
    low = jnp.concatenate([down_in[:half], adapter_down_outputs[:half]], 2)
    high = jnp.concatenate([down_in[half:], adapter_down_outputs[half:]], 2)
    down_factors = ring(low, high)
    base_gate = base_product(pieces, gate_matrix)
    base_up = base_product(pieces, up_matrix)

    tokens_pair = (tokens, swap(tokens))
    tenants = jnp.stack([token_tenant, swap(token_tenant)])
    table = jnp.arange(tenant_storage_slot.shape[0], dtype=jnp.int32)
    match = tenants[:, :, None] == table[None, None, :]
    slot = jnp.sum(jnp.where(match, tenant_storage_slot[None, None, :], 0), 2)
    server = slot // block_slots
    local = slot - server * block_slots
    picks = (server[:, :, None] == jnp.arange(groups, dtype=jnp.int32)).astype(jnp.int32)
    place = jnp.sum(picks * (jnp.cumsum(picks, 1) - 1), 2)
    apart = lax.rem(server // 2 - lax.axis_index("z") + chips, chips)
    turn = jnp.where(apart == 0, 0, jnp.where(apart == chips - 1, 1, jnp.where(apart == 1, 2, 3)))
    seat = turn * capacity + place
    mine = lax.rem(server, 2) == lax.axis_index("c")
    here = jnp.where(mine, seat, -1)
    there = jnp.where(mine, -1, seat)[0]
    seats = jnp.arange(side, dtype=jnp.int32)
    take = (seats[None, :, None] == here[:, None, :]).astype(BF)
    give_here = (here[0][:, None] == seats[None, :]).astype(BF)
    give_there = (there[:, None] == seats[None, :]).astype(BF)

    def by_block(pair):
        packed = [dot_bf(take[g], v).reshape(chips, capacity, -1) for g, v in enumerate(pair)]
        return jnp.concatenate(packed, 1)

    def home(own, other, start):
        stop = start + own.shape[0]
        return dot(give_here[:, start:stop], own) + dot(give_there[:, start:stop], other)

    seat_local = by_block((local[0][:, None].astype(BF), local[1][:, None].astype(BF)))

    seated = by_block(tokens_pair)
    chosen = seat_local.astype(F32) == jnp.arange(block_slots, dtype=F32)[None, None, :]
    parts = []
    for i, f in enumerate(in_factors):
        part = jnp.einsum("ny,eyq->neq", seated[i], f, preferred_element_type=F32)
        parts.append(jnp.sum(part * chosen[i].astype(F32)[:, :, None], 1).astype(BF))
    own = jnp.concatenate([o[:capacity] for o in parts], 0)
    other = swap(jnp.concatenate([o[capacity:] for o in parts], 0))
    home_part = home(own, other, 0).astype(BF)
    ranks = sum_tp(home_part)
    seated_ranks = by_block((ranks, swap(ranks)))

    def deltas(first, last):
        count = last - first
        flops = 4 * 2 * capacity * count * block_slots * rank * hidden_share
        return seated_call(
            delta_kernel,
            rank,
            seated_ranks[first:last],
            seat_local[first:last],
            out_factors[first:last],
            2 * hidden_share,
            flops,
        )

    own, other = deltas(0, chips - 1)
    other = swap(other)
    gate = base_gate + home(own[:, :hidden_share], other[:, :hidden_share], 0)
    up = base_up + home(own[:, hidden_share:], other[:, hidden_share:], 0)
    own, other = deltas(chips - 1, chips)
    other = swap(other)
    gate = gate + home(own[:, :hidden_share], other[:, :hidden_share], near)
    up = up + home(own[:, hidden_share:], other[:, hidden_share:], near)
    hidden = (jax.nn.silu(gate) * up).astype(BF)

    partial = down_product(hidden, down_matrix, lax.axis_size("x"))
    hidden_pair = (hidden, swap(hidden))
    summed = scatter_sum(partial)

    seated_hidden = by_block(hidden_pair)
    flops = 4 * side * block_slots * rank * hidden_share
    own, other = seated_call(
        down_rank_kernel, rank, seated_hidden, seat_local, down_factors, rank, flops
    )
    down_rows = home(own, swap(other), 0).astype(BF)
    down_ranks = sum_tp(down_rows)
    seated_down = by_block((down_ranks, swap(down_ranks)))
    flops = 4 * side * block_slots * rank * width_share
    own, other = seated_call(
        down_delta_kernel, rank, seated_down, seat_local, down_factors, width_share, flops
    )
    returned = home(own, swap(other), 0)
    return (summed + returned).astype(BF)


def solution(mesh):
    sizes = mesh.devices.shape
    cores = 2
    side = 4
    fine = Mesh(
        mesh.devices.reshape(sizes[0] // cores, cores, sizes[1] // side, side),
        ("z", "c", "x", "y"),
    )
    return jax.shard_map(
        layer,
        mesh=fine,
        in_specs=(
            P(GRP, TP),
            P(GRP),
            P(),
            P(None, TP),
            P(None, TP),
            P(TP, None),
            P(GRP, TP, None),
            P(GRP, None, TP),
            P(GRP, TP, None),
            P(GRP, None, TP),
        ),
        out_specs=P(GRP, TP),
        check_vma=False,
    )
```

```python
import functools

import jax
import jax.numpy as jnp
from jax import lax
from jax.experimental import pallas as pl
from jax.experimental.pallas import tpu as pltpu
from jax.sharding import Mesh, PartitionSpec as P

GRP = ("z", "c")
TP = ("x", "y")
BF = jnp.bfloat16
F32 = jnp.float32


def dot(a, b):
    return jnp.dot(a, b, preferred_element_type=F32)


def dot_bf(a, b):
    return dot(a, b).astype(BF)


def shift(values, axis, step):
    n = lax.axis_size(axis)
    return lax.ppermute(values, axis, [(i, (i + step) % n) for i in range(n)])


def swap(values):
    return shift(values, "c", 1)


def sum_over(values, axis):
    got = [shift(values, axis, step).astype(F32) for step in (1, -1, 2)]
    return ((values.astype(F32) + got[0]) + (got[1] + got[2])).astype(BF)


def sum_tp(values):
    first = sum_over(values, "x")
    return sum_over(first, "y")


def ring(first, second):
    below = (shift(first, "z", 1), shift(second, "z", 1))
    above = (shift(first, "z", -1), shift(second, "z", -1))
    far = (shift(below[0], "z", 1), shift(above[1], "z", -1))
    return [(first, second), below, above, far]


def base_kernel(order, a_ref, b_ref, wa_ref, wb_ref, out_ref):
    n, _, part = a_ref.shape[1:]
    pieces = [a_ref[0, order[2 * n + i]] for i in range(n)]
    pieces += [b_ref[0, order[3 * n + i]] for i in range(n)]
    width = wa_ref.shape[-1]
    wa = wa_ref[...].reshape(n * part, width)
    wb = wb_ref[...].reshape(n * part, width)
    product = dot(jnp.concatenate(pieces, 1), jnp.concatenate([wa, wb], 0))
    first = pl.program_id(0) == 0

    @pl.when(first)
    def _():
        out_ref[...] = product

    @pl.when(jnp.logical_not(first))
    def _():
        out_ref[...] += product


def peers(values, axis):
    return jnp.stack([values] + [shift(values, axis, step) for step in (1, -1, 2)])


def index_order(axis, sign):
    n = lax.axis_size(axis)
    which = jnp.arange(n, dtype=jnp.int32)
    step = jnp.where(which == 0, 0, jnp.where(which == 1, 1, jnp.where(which == 2, -1, 2)))
    return lax.rem(lax.axis_index(axis) + sign * step + n, n).astype(jnp.int32)


def place_order(axis):
    n = lax.axis_size(axis)
    apart = lax.rem(lax.axis_index(axis) - jnp.arange(n, dtype=jnp.int32) + n, n)
    return jnp.where(apart == 0, 0, jnp.where(apart == 1, 1, jnp.where(apart == n - 1, 2, 3)))


def gather_tokens(tokens):
    part = tokens.shape[1] // 2
    a_line = peers(tokens[:, :part], "x")
    b_line = peers(tokens[:, part:], "y")
    return peers(a_line, "y"), peers(b_line, "x")


def base_product(pieces, matrix):
    a_all, b_all = pieces
    n, _, rows, part = a_all.shape
    width = matrix.shape[1]
    order = jnp.concatenate(
        [index_order("y", -1), index_order("x", -1), place_order("x"), place_order("y")]
    )
    weights = matrix.reshape(n, n, 2, part, width)
    line = pl.BlockSpec((1, n, rows, part), lambda k, o: (k, 0, 0, 0))
    grid_spec = pltpu.PrefetchScalarGridSpec(
        num_scalar_prefetch=1,
        grid=(n,),
        in_specs=[
            line,
            line,
            pl.BlockSpec((n, 1, 1, part, width), lambda k, o: (0, o[k], 0, 0, 0)),
            pl.BlockSpec((1, n, 1, part, width), lambda k, o: (o[n + k], 0, 1, 0, 0)),
        ],
        out_specs=pl.BlockSpec((rows, width), lambda k, o: (0, 0)),
    )
    return pl.pallas_call(
        base_kernel,
        grid_spec=grid_spec,
        out_shape=jax.ShapeDtypeStruct((rows, width), F32),
        name="base",
        compiler_params=pltpu.CompilerParams(vmem_limit_bytes=16 << 20),
        cost_estimate=pl.CostEstimate(
            flops=2 * rows * matrix.size,
            bytes_accessed=2 * matrix.size + 2 * a_all.size + 2 * b_all.size + 4 * rows * width,
            transcendentals=0,
        ),
    )(order, a_all, b_all, weights, weights)


def down_kernel(order, hidden_ref, w_ref, *outs):
    n = len(outs) // 2
    half, span = outs[0].shape
    share = span // n
    step = pl.program_id(0)
    starts = [pl.multiple_of(order[n + m] * share, share) for m in range(n)]
    weights = jnp.concatenate([w_ref[:, pl.ds(start, share)] for start in starts], 1)
    product = dot_bf(hidden_ref[...], weights)
    for m in range(n):
        place = pl.ds(pl.multiple_of(step * share, share), share)
        outs[n + m][:, place] = product[half:, m * share : (m + 1) * share]
    for k in range(n):

        @pl.when(step == k)
        def _(k=k):
            outs[k][...] = product[:half]


def down_product(hidden, matrix, n):
    rows, depth = hidden.shape
    span = matrix.shape[1] // n
    order = jnp.concatenate([index_order("x", 1), index_order("y", 1)])
    grid_spec = pltpu.PrefetchScalarGridSpec(
        num_scalar_prefetch=1,
        grid=(n,),
        in_specs=[
            pl.BlockSpec((rows, depth), lambda k, o: (0, 0)),
            pl.BlockSpec((depth, span), lambda k, o: (0, o[k])),
        ],
        out_specs=[pl.BlockSpec((rows // 2, span), lambda k, o: (0, 0))] * (2 * n),
    )
    outs = pl.pallas_call(
        down_kernel,
        grid_spec=grid_spec,
        out_shape=[jax.ShapeDtypeStruct((rows // 2, span), BF)] * (2 * n),
        name="partial",
        compiler_params=pltpu.CompilerParams(vmem_limit_bytes=18 << 20),
        cost_estimate=pl.CostEstimate(
            flops=2 * rows * matrix.size,
            bytes_accessed=2 * matrix.size + 2 * hidden.size + 2 * rows * matrix.shape[1],
            transcendentals=0,
        ),
    )(order, hidden, matrix)
    return outs[:n], outs[n:]


def scatter_over(parts, axis):
    got = [shift(part, axis, step).astype(F32) for part, step in zip(parts[1:], (1, -1, 2))]
    return (parts[0].astype(F32) + got[0]) + (got[1] + got[2])


def scatter_sum(parts):
    low, high = parts
    n = len(low)
    low = scatter_over(low, "x").astype(BF)
    high = scatter_over(high, "y").astype(BF)
    low = scatter_over(jnp.split(low, n, 1), "y")
    high = scatter_over(jnp.split(high, n, 1), "x")
    return jnp.concatenate([low, high], 0)


def fan_out(start, depth, rank, slots):
    lane = lax.broadcasted_iota(jnp.int32, (depth, slots * rank), 1)
    row = lax.broadcasted_iota(jnp.int32, (depth, slots * rank), 0)
    return (row == lax.rem(lane, rank) + start).astype(BF)


def slot_mask(local, rows, rank, first, slots):
    lane = lax.broadcasted_iota(jnp.int32, (rows, slots * rank), 1) // rank + first
    return local.astype(F32).astype(jnp.int32) == lane


def split_rows(values, own_ref, other_ref, i):
    half = values.shape[0] // 2
    rows = pl.ds(i * half, half)
    return (own_ref, rows, values[:half]), (other_ref, rows, values[half:])


def delta_kernel(count, rank, *refs):
    ranks_ref, local_ref = refs[:2]
    factors = refs[2 : 2 + 2 * count]
    own_ref, other_ref = refs[2 + 2 * count :]
    slots = factors[0].shape[0]
    width = factors[0].shape[2]
    rows = ranks_ref.shape[1]
    for which in range(2):
        fan = fan_out(which * rank, ranks_ref.shape[2], rank, slots)
        for i in range(count):
            wide = dot(ranks_ref[i], fan)
            wide = jnp.where(slot_mask(local_ref[i], rows, rank, 0, slots), wide, 0.0).astype(BF)
            delta = dot_bf(wide, factors[2 * i + which][...].reshape(slots * rank, width))
            for ref, at, part in split_rows(delta, own_ref, other_ref, i):
                ref[at, which * width : (which + 1) * width] = part


def down_rank_kernel(count, rank, *refs):
    hidden_ref, local_ref = refs[:2]
    factors = refs[2 : 2 + 2 * count]
    own_ref, other_ref = refs[2 + 2 * count :]
    slots = factors[0].shape[0]
    rows, depth = hidden_ref.shape[1:]
    fan = fan_out(0, rank, rank, slots)
    for i in range(count):
        total = jnp.zeros((rows, rank), F32)
        for which in range(2):
            factor = factors[2 * i + which][:, :, :depth].reshape(slots * rank, depth)
            part = lax.dot_general(
                hidden_ref[i], factor, (((1,), (1,)), ((), ())), preferred_element_type=F32
            )
            mask = slot_mask(local_ref[i], rows, rank, which * slots, slots)
            part = jnp.where(mask, part, 0.0).astype(BF)
            total += lax.dot_general(part, fan, (((1,), (1,)), ((), ())), preferred_element_type=F32)
        for ref, at, part in split_rows(total.astype(BF), own_ref, other_ref, i):
            ref[at, :] = part


def down_delta_kernel(count, rank, *refs):
    ranks_ref, local_ref = refs[:2]
    factors = refs[2 : 2 + 2 * count]
    own_ref, other_ref = refs[2 + 2 * count :]
    slots = factors[0].shape[0]
    rows = ranks_ref.shape[1]
    width = own_ref.shape[1]
    fan = fan_out(0, rank, rank, slots)
    for i in range(count):
        total = jnp.zeros((rows, width), F32)
        spread = dot(ranks_ref[i], fan)
        for which in range(2):
            mask = slot_mask(local_ref[i], rows, rank, which * slots, slots)
            wide = jnp.where(mask, spread, 0.0).astype(BF)
            factor = factors[2 * i + which]
            factor = factor[:, :, factor.shape[2] - width :].reshape(slots * rank, width)
            total += dot(wide, factor)
        for ref, at, part in split_rows(total.astype(BF), own_ref, other_ref, i):
            ref[at, :] = part


def seated_call(kernel, rank, seated, local, factors, width, flops):
    count, rows = seated.shape[:2]
    out = jax.ShapeDtypeStruct((count * rows // 2, width), BF)
    flat = [f for pair in factors for f in pair]
    moved = sum(2 * f.size for f in flat) + 4 * out.size + 2 * seated.size
    return pl.pallas_call(
        functools.partial(kernel, count, rank),
        in_specs=[pl.BlockSpec(memory_space=pltpu.VMEM)] * (2 + len(flat)),
        out_specs=[pl.BlockSpec(memory_space=pltpu.VMEM)] * 2,
        out_shape=[out, out],
        compiler_params=pltpu.CompilerParams(vmem_limit_bytes=16 << 20),
        cost_estimate=pl.CostEstimate(flops=flops, bytes_accessed=moved, transcendentals=0),
    )(seated, local, *flat)


def layer(
    tokens,
    token_tenant,
    tenant_storage_slot,
    gate_matrix,
    up_matrix,
    down_matrix,
    adapter_gate_up_inputs,
    adapter_gate_up_outputs,
    adapter_down_inputs,
    adapter_down_outputs,
):
    groups = lax.axis_size(GRP)
    rows = tokens.shape[0]
    block_slots = adapter_gate_up_inputs.shape[0]
    rank = adapter_gate_up_inputs.shape[2] // 2
    hidden_share = gate_matrix.shape[1]
    width_share = tokens.shape[1]
    capacity = 2 * rows // groups
    chips = groups // 2
    side = chips * capacity
    near = (chips - 1) * capacity

    in_factors = [adapter_gate_up_inputs]
    in_factors += [shift(adapter_gate_up_inputs, "z", step) for step in (1, -1, 2)]
    pieces = gather_tokens(tokens)
    gate_part = adapter_gate_up_outputs[:, :rank, :]
    up_part = adapter_gate_up_outputs[:, rank:, :]
    out_factors = ring(gate_part, up_part)
    down_in = adapter_down_inputs.swapaxes(1, 2)
    half = block_slots // 2
    low = jnp.concatenate([down_in[:half], adapter_down_outputs[:half]], 2)
    high = jnp.concatenate([down_in[half:], adapter_down_outputs[half:]], 2)
    down_factors = ring(low, high)
    base_gate = base_product(pieces, gate_matrix)
    base_up = base_product(pieces, up_matrix)

    tokens_pair = (tokens, swap(tokens))
    tenants = jnp.stack([token_tenant, swap(token_tenant)])
    table = jnp.arange(tenant_storage_slot.shape[0], dtype=jnp.int32)
    match = tenants[:, :, None] == table[None, None, :]
    slot = jnp.sum(jnp.where(match, tenant_storage_slot[None, None, :], 0), 2)
    server = slot // block_slots
    local = slot - server * block_slots
    picks = (server[:, :, None] == jnp.arange(groups, dtype=jnp.int32)).astype(jnp.int32)
    place = jnp.sum(picks * (jnp.cumsum(picks, 1) - 1), 2)
    apart = lax.rem(server // 2 - lax.axis_index("z") + chips, chips)
    turn = jnp.where(apart == 0, 0, jnp.where(apart == chips - 1, 1, jnp.where(apart == 1, 2, 3)))
    seat = turn * capacity + place
    mine = lax.rem(server, 2) == lax.axis_index("c")
    here = jnp.where(mine, seat, -1)
    there = jnp.where(mine, -1, seat)[0]
    seats = jnp.arange(side, dtype=jnp.int32)
    take = (seats[None, :, None] == here[:, None, :]).astype(BF)
    give_here = (here[0][:, None] == seats[None, :]).astype(BF)
    give_there = (there[:, None] == seats[None, :]).astype(BF)

    def by_block(pair):
        packed = [dot_bf(take[g], v).reshape(chips, capacity, -1) for g, v in enumerate(pair)]
        return jnp.concatenate(packed, 1)

    def home(own, other, start):
        stop = start + own.shape[0]
        return dot(give_here[:, start:stop], own) + dot(give_there[:, start:stop], other)

    seat_local = by_block((local[0][:, None].astype(BF), local[1][:, None].astype(BF)))

    seated = by_block(tokens_pair)
    chosen = seat_local.astype(F32) == jnp.arange(block_slots, dtype=F32)[None, None, :]
    parts = []
    for i, f in enumerate(in_factors):
        part = jnp.einsum("ny,eyq->neq", seated[i], f, preferred_element_type=F32)
        parts.append(jnp.sum(part * chosen[i].astype(F32)[:, :, None], 1).astype(BF))
    own = jnp.concatenate([o[:capacity] for o in parts], 0)
    other = swap(jnp.concatenate([o[capacity:] for o in parts], 0))
    home_part = home(own, other, 0).astype(BF)
    ranks = sum_tp(home_part)
    seated_ranks = by_block((ranks, swap(ranks)))

    def deltas(first, last):
        count = last - first
        flops = 4 * 2 * capacity * count * block_slots * rank * hidden_share
        return seated_call(
            delta_kernel,
            rank,
            seated_ranks[first:last],
            seat_local[first:last],
            out_factors[first:last],
            2 * hidden_share,
            flops,
        )

    own, other = deltas(0, chips - 1)
    other = swap(other)
    gate = base_gate + home(own[:, :hidden_share], other[:, :hidden_share], 0)
    up = base_up + home(own[:, hidden_share:], other[:, hidden_share:], 0)
    own, other = deltas(chips - 1, chips)
    other = swap(other)
    gate = gate + home(own[:, :hidden_share], other[:, :hidden_share], near)
    up = up + home(own[:, hidden_share:], other[:, hidden_share:], near)
    hidden = (jax.nn.silu(gate) * up).astype(BF)

    partial = down_product(hidden, down_matrix, lax.axis_size("x"))
    hidden_pair = (hidden, swap(hidden))
    summed = scatter_sum(partial)

    seated_hidden = by_block(hidden_pair)
    flops = 4 * side * block_slots * rank * hidden_share
    own, other = seated_call(
        down_rank_kernel, rank, seated_hidden, seat_local, down_factors, rank, flops
    )
    down_rows = home(own, swap(other), 0).astype(BF)
    down_ranks = sum_tp(down_rows)
    seated_down = by_block((down_ranks, swap(down_ranks)))
    flops = 4 * side * block_slots * rank * width_share
    own, other = seated_call(
        down_delta_kernel, rank, seated_down, seat_local, down_factors, width_share, flops
    )
    returned = home(own, swap(other), 0)
    return (summed + returned).astype(BF)


def solution(mesh):
    sizes = mesh.devices.shape
    cores = 2
    side = 4
    fine = Mesh(
        mesh.devices.reshape(sizes[0] // cores, cores, sizes[1] // side, side),
        ("z", "c", "x", "y"),
    )
    return jax.shard_map(
        layer,
        mesh=fine,
        in_specs=(
            P(GRP, TP),
            P(GRP),
            P(),
            P(None, TP),
            P(None, TP),
            P(TP, None),
            P(GRP, TP, None),
            P(GRP, None, TP),
            P(GRP, TP, None),
            P(GRP, None, TP),
        ),
        out_specs=P(GRP, TP),
        check_vma=False,
    )
```

```python
import functools

import jax
import jax.numpy as jnp
from jax import lax
from jax.experimental import pallas as pl
from jax.experimental.pallas import tpu as pltpu
from jax.sharding import Mesh, PartitionSpec as P

GRP = ("z", "c")
TP = ("x", "y")
BF = jnp.bfloat16
F32 = jnp.float32


def dot(a, b):
    return jnp.dot(a, b, preferred_element_type=F32)


def dot_bf(a, b):
    return dot(a, b).astype(BF)


def shift(values, axis, step):
    n = lax.axis_size(axis)
    return lax.ppermute(values, axis, [(i, (i + step) % n) for i in range(n)])


def swap(values):
    return shift(values, "c", 1)


def sum_over(values, axis):
    got = [shift(values, axis, step).astype(F32) for step in (1, -1, 2)]
    return ((values.astype(F32) + got[0]) + (got[1] + got[2])).astype(BF)


def sum_tp(values):
    first = sum_over(values, "x")
    return sum_over(first, "y")


def ring(first, second):
    below = (shift(first, "z", 1), shift(second, "z", 1))
    above = (shift(first, "z", -1), shift(second, "z", -1))
    far = (shift(below[0], "z", 1), shift(above[1], "z", -1))
    return [(first, second), below, above, far]


def base_kernel(order, a_ref, b_ref, wa_ref, wb_ref, out_ref):
    n, _, part = a_ref.shape[1:]
    pieces = [a_ref[0, order[2 * n + i]] for i in range(n)]
    pieces += [b_ref[0, order[3 * n + i]] for i in range(n)]
    width = wa_ref.shape[-1]
    wa = wa_ref[...].reshape(n * part, width)
    wb = wb_ref[...].reshape(n * part, width)
    product = dot(jnp.concatenate(pieces, 1), jnp.concatenate([wa, wb], 0))
    first = pl.program_id(0) == 0

    @pl.when(first)
    def _():
        out_ref[...] = product

    @pl.when(jnp.logical_not(first))
    def _():
        out_ref[...] += product


def peers(values, axis):
    return jnp.stack([values] + [shift(values, axis, step) for step in (1, -1, 2)])


def index_order(axis, sign):
    n = lax.axis_size(axis)
    which = jnp.arange(n, dtype=jnp.int32)
    step = jnp.where(which == 0, 0, jnp.where(which == 1, 1, jnp.where(which == 2, -1, 2)))
    return lax.rem(lax.axis_index(axis) + sign * step + n, n).astype(jnp.int32)


def place_order(axis):
    n = lax.axis_size(axis)
    apart = lax.rem(lax.axis_index(axis) - jnp.arange(n, dtype=jnp.int32) + n, n)
    return jnp.where(apart == 0, 0, jnp.where(apart == 1, 1, jnp.where(apart == n - 1, 2, 3)))


def gather_tokens(tokens):
    part = tokens.shape[1] // 2
    a_line = peers(tokens[:, :part], "x")
    b_line = peers(tokens[:, part:], "y")
    return peers(a_line, "y"), peers(b_line, "x")


def base_product(pieces, matrix):
    a_all, b_all = pieces
    n, _, rows, part = a_all.shape
    width = matrix.shape[1]
    order = jnp.concatenate(
        [index_order("y", -1), index_order("x", -1), place_order("x"), place_order("y")]
    )
    weights = matrix.reshape(n, n, 2, part, width)
    line = pl.BlockSpec((1, n, rows, part), lambda k, o: (k, 0, 0, 0))
    grid_spec = pltpu.PrefetchScalarGridSpec(
        num_scalar_prefetch=1,
        grid=(n,),
        in_specs=[
            line,
            line,
            pl.BlockSpec((n, 1, 1, part, width), lambda k, o: (0, o[k], 0, 0, 0)),
            pl.BlockSpec((1, n, 1, part, width), lambda k, o: (o[n + k], 0, 1, 0, 0)),
        ],
        out_specs=pl.BlockSpec((rows, width), lambda k, o: (0, 0)),
    )
    return pl.pallas_call(
        base_kernel,
        grid_spec=grid_spec,
        out_shape=jax.ShapeDtypeStruct((rows, width), F32),
        name="base",
        compiler_params=pltpu.CompilerParams(vmem_limit_bytes=10 << 20),
        cost_estimate=pl.CostEstimate(
            flops=2 * rows * matrix.size,
            bytes_accessed=2 * matrix.size + 2 * a_all.size + 2 * b_all.size + 4 * rows * width,
            transcendentals=0,
        ),
    )(order, a_all, b_all, weights, weights)


def down_kernel(order, hidden_ref, w_ref, *outs):
    n = len(outs) // 2
    half, span = outs[0].shape
    share = span // n
    step = pl.program_id(0)
    starts = [pl.multiple_of(order[n + m] * share, share) for m in range(n)]
    weights = jnp.concatenate([w_ref[:, pl.ds(start, share)] for start in starts], 1)
    product = dot_bf(hidden_ref[...], weights)
    for m in range(n):
        place = pl.ds(pl.multiple_of(step * share, share), share)
        outs[n + m][:, place] = product[half:, m * share : (m + 1) * share]
    for k in range(n):

        @pl.when(step == k)
        def _(k=k):
            outs[k][...] = product[:half]


def down_product(hidden, matrix, n):
    rows, depth = hidden.shape
    span = matrix.shape[1] // n
    order = jnp.concatenate([index_order("x", 1), index_order("y", 1)])
    grid_spec = pltpu.PrefetchScalarGridSpec(
        num_scalar_prefetch=1,
        grid=(n,),
        in_specs=[
            pl.BlockSpec((rows, depth), lambda k, o: (0, 0)),
            pl.BlockSpec((depth, span), lambda k, o: (0, o[k])),
        ],
        out_specs=[pl.BlockSpec((rows // 2, span), lambda k, o: (0, 0))] * (2 * n),
    )
    outs = pl.pallas_call(
        down_kernel,
        grid_spec=grid_spec,
        out_shape=[jax.ShapeDtypeStruct((rows // 2, span), BF)] * (2 * n),
        name="partial",
        compiler_params=pltpu.CompilerParams(vmem_limit_bytes=10 << 20),
        cost_estimate=pl.CostEstimate(
            flops=2 * rows * matrix.size,
            bytes_accessed=2 * matrix.size + 2 * hidden.size + 2 * rows * matrix.shape[1],
            transcendentals=0,
        ),
    )(order, hidden, matrix)
    return outs[:n], outs[n:]


def scatter_over(parts, axis):
    got = [shift(part, axis, step).astype(F32) for part, step in zip(parts[1:], (1, -1, 2))]
    return (parts[0].astype(F32) + got[0]) + (got[1] + got[2])


def scatter_sum(parts):
    low, high = parts
    n = len(low)
    low = scatter_over(low, "x").astype(BF)
    high = scatter_over(high, "y").astype(BF)
    low = scatter_over(jnp.split(low, n, 1), "y")
    high = scatter_over(jnp.split(high, n, 1), "x")
    return jnp.concatenate([low, high], 0)


def fan_out(start, depth, rank, slots):
    lane = lax.broadcasted_iota(jnp.int32, (depth, slots * rank), 1)
    row = lax.broadcasted_iota(jnp.int32, (depth, slots * rank), 0)
    return (row == lax.rem(lane, rank) + start).astype(BF)


def slot_mask(local, rows, rank, first, slots):
    lane = lax.broadcasted_iota(jnp.int32, (rows, slots * rank), 1) // rank + first
    return local.astype(F32).astype(jnp.int32) == lane


def split_rows(values, own_ref, other_ref, i):
    half = values.shape[0] // 2
    rows = pl.ds(i * half, half)
    return (own_ref, rows, values[:half]), (other_ref, rows, values[half:])


def delta_kernel(count, rank, *refs):
    ranks_ref, local_ref = refs[:2]
    factors = refs[2 : 2 + 2 * count]
    own_ref, other_ref = refs[2 + 2 * count :]
    slots = factors[0].shape[0]
    width = factors[0].shape[2]
    rows = ranks_ref.shape[1]
    for which in range(2):
        fan = fan_out(which * rank, ranks_ref.shape[2], rank, slots)
        for i in range(count):
            wide = dot(ranks_ref[i], fan)
            wide = jnp.where(slot_mask(local_ref[i], rows, rank, 0, slots), wide, 0.0).astype(BF)
            delta = dot_bf(wide, factors[2 * i + which][...].reshape(slots * rank, width))
            for ref, at, part in split_rows(delta, own_ref, other_ref, i):
                ref[at, which * width : (which + 1) * width] = part


def down_rank_kernel(count, rank, *refs):
    hidden_ref, local_ref = refs[:2]
    factors = refs[2 : 2 + 2 * count]
    own_ref, other_ref = refs[2 + 2 * count :]
    slots = factors[0].shape[0]
    rows, depth = hidden_ref.shape[1:]
    fan = fan_out(0, rank, rank, slots)
    for i in range(count):
        total = jnp.zeros((rows, rank), F32)
        for which in range(2):
            factor = factors[2 * i + which][:, :, :depth].reshape(slots * rank, depth)
            part = lax.dot_general(
                hidden_ref[i], factor, (((1,), (1,)), ((), ())), preferred_element_type=F32
            )
            mask = slot_mask(local_ref[i], rows, rank, which * slots, slots)
            part = jnp.where(mask, part, 0.0).astype(BF)
            total += lax.dot_general(part, fan, (((1,), (1,)), ((), ())), preferred_element_type=F32)
        for ref, at, part in split_rows(total.astype(BF), own_ref, other_ref, i):
            ref[at, :] = part


def down_delta_kernel(count, rank, *refs):
    ranks_ref, local_ref = refs[:2]
    factors = refs[2 : 2 + 2 * count]
    own_ref, other_ref = refs[2 + 2 * count :]
    slots = factors[0].shape[0]
    rows = ranks_ref.shape[1]
    width = own_ref.shape[1]
    fan = fan_out(0, rank, rank, slots)
    for i in range(count):
        total = jnp.zeros((rows, width), F32)
        spread = dot(ranks_ref[i], fan)
        for which in range(2):
            mask = slot_mask(local_ref[i], rows, rank, which * slots, slots)
            wide = jnp.where(mask, spread, 0.0).astype(BF)
            factor = factors[2 * i + which]
            factor = factor[:, :, factor.shape[2] - width :].reshape(slots * rank, width)
            total += dot(wide, factor)
        for ref, at, part in split_rows(total.astype(BF), own_ref, other_ref, i):
            ref[at, :] = part


def seated_call(kernel, rank, seated, local, factors, width, flops):
    count, rows = seated.shape[:2]
    out = jax.ShapeDtypeStruct((count * rows // 2, width), BF)
    flat = [f for pair in factors for f in pair]
    moved = sum(2 * f.size for f in flat) + 4 * out.size + 2 * seated.size
    return pl.pallas_call(
        functools.partial(kernel, count, rank),
        in_specs=[pl.BlockSpec(memory_space=pltpu.VMEM)] * (2 + len(flat)),
        out_specs=[pl.BlockSpec(memory_space=pltpu.VMEM)] * 2,
        out_shape=[out, out],
        compiler_params=pltpu.CompilerParams(vmem_limit_bytes=9 << 20),
        cost_estimate=pl.CostEstimate(flops=flops, bytes_accessed=moved, transcendentals=0),
    )(seated, local, *flat)


def layer(
    tokens,
    token_tenant,
    tenant_storage_slot,
    gate_matrix,
    up_matrix,
    down_matrix,
    adapter_gate_up_inputs,
    adapter_gate_up_outputs,
    adapter_down_inputs,
    adapter_down_outputs,
):
    groups = lax.axis_size(GRP)
    rows = tokens.shape[0]
    block_slots = adapter_gate_up_inputs.shape[0]
    rank = adapter_gate_up_inputs.shape[2] // 2
    hidden_share = gate_matrix.shape[1]
    width_share = tokens.shape[1]
    capacity = 2 * rows // groups
    chips = groups // 2
    side = chips * capacity
    near = (chips - 1) * capacity

    in_factors = [adapter_gate_up_inputs]
    in_factors += [shift(adapter_gate_up_inputs, "z", step) for step in (1, -1, 2)]
    pieces = gather_tokens(tokens)
    gate_part = adapter_gate_up_outputs[:, :rank, :]
    up_part = adapter_gate_up_outputs[:, rank:, :]
    out_factors = ring(gate_part, up_part)
    down_in = adapter_down_inputs.swapaxes(1, 2)
    half = block_slots // 2
    low = jnp.concatenate([down_in[:half], adapter_down_outputs[:half]], 2)
    high = jnp.concatenate([down_in[half:], adapter_down_outputs[half:]], 2)
    down_factors = ring(low, high)
    base_gate = base_product(pieces, gate_matrix)
    base_up = base_product(pieces, up_matrix)

    tokens_pair = (tokens, swap(tokens))
    tenants = jnp.stack([token_tenant, swap(token_tenant)])
    table = jnp.arange(tenant_storage_slot.shape[0], dtype=jnp.int32)
    match = tenants[:, :, None] == table[None, None, :]
    slot = jnp.sum(jnp.where(match, tenant_storage_slot[None, None, :], 0), 2)
    server = slot // block_slots
    local = slot - server * block_slots
    picks = (server[:, :, None] == jnp.arange(groups, dtype=jnp.int32)).astype(jnp.int32)
    place = jnp.sum(picks * (jnp.cumsum(picks, 1) - 1), 2)
    apart = lax.rem(server // 2 - lax.axis_index("z") + chips, chips)
    turn = jnp.where(apart == 0, 0, jnp.where(apart == chips - 1, 1, jnp.where(apart == 1, 2, 3)))
    seat = turn * capacity + place
    mine = lax.rem(server, 2) == lax.axis_index("c")
    here = jnp.where(mine, seat, -1)
    there = jnp.where(mine, -1, seat)[0]
    seats = jnp.arange(side, dtype=jnp.int32)
    take = (seats[None, :, None] == here[:, None, :]).astype(BF)
    give_here = (here[0][:, None] == seats[None, :]).astype(BF)
    give_there = (there[:, None] == seats[None, :]).astype(BF)

    def by_block(pair):
        packed = [dot_bf(take[g], v).reshape(chips, capacity, -1) for g, v in enumerate(pair)]
        return jnp.concatenate(packed, 1)

    def home(own, other, start):
        stop = start + own.shape[0]
        return dot(give_here[:, start:stop], own) + dot(give_there[:, start:stop], other)

    seat_local = by_block((local[0][:, None].astype(BF), local[1][:, None].astype(BF)))

    seated = by_block(tokens_pair)
    chosen = seat_local.astype(F32) == jnp.arange(block_slots, dtype=F32)[None, None, :]
    parts = []
    for i, f in enumerate(in_factors):
        part = jnp.einsum("ny,eyq->neq", seated[i], f, preferred_element_type=F32)
        parts.append(jnp.sum(part * chosen[i].astype(F32)[:, :, None], 1).astype(BF))
    own = jnp.concatenate([o[:capacity] for o in parts], 0)
    other = swap(jnp.concatenate([o[capacity:] for o in parts], 0))
    home_part = home(own, other, 0).astype(BF)
    ranks = sum_tp(home_part)
    seated_ranks = by_block((ranks, swap(ranks)))

    def deltas(first, last):
        count = last - first
        flops = 4 * 2 * capacity * count * block_slots * rank * hidden_share
        return seated_call(
            delta_kernel,
            rank,
            seated_ranks[first:last],
            seat_local[first:last],
            out_factors[first:last],
            2 * hidden_share,
            flops,
        )

    own, other = deltas(0, chips - 1)
    other = swap(other)
    gate = base_gate + home(own[:, :hidden_share], other[:, :hidden_share], 0)
    up = base_up + home(own[:, hidden_share:], other[:, hidden_share:], 0)
    own, other = deltas(chips - 1, chips)
    other = swap(other)
    gate = gate + home(own[:, :hidden_share], other[:, :hidden_share], near)
    up = up + home(own[:, hidden_share:], other[:, hidden_share:], near)
    hidden = (jax.nn.silu(gate) * up).astype(BF)

    partial = down_product(hidden, down_matrix, lax.axis_size("x"))
    hidden_pair = (hidden, swap(hidden))
    summed = scatter_sum(partial)

    seated_hidden = by_block(hidden_pair)
    flops = 4 * side * block_slots * rank * hidden_share
    own, other = seated_call(
        down_rank_kernel, rank, seated_hidden, seat_local, down_factors, rank, flops
    )
    down_rows = home(own, swap(other), 0).astype(BF)
    down_ranks = sum_tp(down_rows)
    seated_down = by_block((down_ranks, swap(down_ranks)))
    flops = 4 * side * block_slots * rank * width_share
    own, other = seated_call(
        down_delta_kernel, rank, seated_down, seat_local, down_factors, width_share, flops
    )
    returned = home(own, swap(other), 0)
    return (summed + returned).astype(BF)


def solution(mesh):
    sizes = mesh.devices.shape
    cores = 2
    side = 4
    fine = Mesh(
        mesh.devices.reshape(sizes[0] // cores, cores, sizes[1] // side, side),
        ("z", "c", "x", "y"),
    )
    return jax.shard_map(
        layer,
        mesh=fine,
        in_specs=(
            P(GRP, TP),
            P(GRP),
            P(),
            P(None, TP),
            P(None, TP),
            P(TP, None),
            P(GRP, TP, None),
            P(GRP, None, TP),
            P(GRP, TP, None),
            P(GRP, None, TP),
        ),
        out_specs=P(GRP, TP),
        check_vma=False,
    )
```

```python
import functools

import jax
import jax.numpy as jnp
from jax import lax
from jax.experimental import pallas as pl
from jax.experimental.pallas import tpu as pltpu
from jax.sharding import Mesh, PartitionSpec as P

GRP = ("z", "c")
TP = ("x", "y")
BF = jnp.bfloat16
F32 = jnp.float32


def dot(a, b):
    return jnp.dot(a, b, preferred_element_type=F32)


def dot_bf(a, b):
    return dot(a, b).astype(BF)


def shift(values, axis, step):
    n = lax.axis_size(axis)
    return lax.ppermute(values, axis, [(i, (i + step) % n) for i in range(n)])


def swap(values):
    return shift(values, "c", 1)


def sum_over(values, axis):
    n = lax.axis_size(axis)
    many = jnp.broadcast_to(values[None], (n,) + values.shape)
    got = lax.all_to_all(many, axis, split_axis=0, concat_axis=0, tiled=True)
    return jnp.sum(got.astype(F32), 0).astype(BF)


def sum_tp(values):
    first = sum_over(values, "x")
    return sum_over(first, "y")


def ring(first, second):
    below = (shift(first, "z", 1), shift(second, "z", 1))
    above = (shift(first, "z", -1), shift(second, "z", -1))
    far = (shift(below[0], "z", 1), shift(above[1], "z", -1))
    return [(first, second), below, above, far]


def base_kernel(order, a_ref, b_ref, wa_ref, wb_ref, out_ref):
    n, _, part = a_ref.shape[1:]
    pieces = [a_ref[0, order[2 * n + i]] for i in range(n)]
    pieces += [b_ref[0, order[3 * n + i]] for i in range(n)]
    width = wa_ref.shape[-1]
    wa = wa_ref[...].reshape(n * part, width)
    wb = wb_ref[...].reshape(n * part, width)
    product = dot(jnp.concatenate(pieces, 1), jnp.concatenate([wa, wb], 0))
    first = pl.program_id(0) == 0

    @pl.when(first)
    def _():
        out_ref[...] = product

    @pl.when(jnp.logical_not(first))
    def _():
        out_ref[...] += product


def peers(values, axis):
    return jnp.stack([values] + [shift(values, axis, step) for step in (1, -1, 2)])


def index_order(axis, sign):
    n = lax.axis_size(axis)
    which = jnp.arange(n, dtype=jnp.int32)
    step = jnp.where(which == 0, 0, jnp.where(which == 1, 1, jnp.where(which == 2, -1, 2)))
    return lax.rem(lax.axis_index(axis) + sign * step + n, n).astype(jnp.int32)


def place_order(axis):
    n = lax.axis_size(axis)
    apart = lax.rem(lax.axis_index(axis) - jnp.arange(n, dtype=jnp.int32) + n, n)
    return jnp.where(apart == 0, 0, jnp.where(apart == 1, 1, jnp.where(apart == n - 1, 2, 3)))


def gather_tokens(tokens):
    part = tokens.shape[1] // 2
    a_line = peers(tokens[:, :part], "x")
    b_line = peers(tokens[:, part:], "y")
    return peers(a_line, "y"), peers(b_line, "x")


def base_product(pieces, matrix):
    a_all, b_all = pieces
    n, _, rows, part = a_all.shape
    width = matrix.shape[1]
    order = jnp.concatenate(
        [index_order("y", -1), index_order("x", -1), place_order("x"), place_order("y")]
    )
    weights = matrix.reshape(n, n, 2, part, width)
    line = pl.BlockSpec((1, n, rows, part), lambda k, o: (k, 0, 0, 0))
    grid_spec = pltpu.PrefetchScalarGridSpec(
        num_scalar_prefetch=1,
        grid=(n,),
        in_specs=[
            line,
            line,
            pl.BlockSpec((n, 1, 1, part, width), lambda k, o: (0, o[k], 0, 0, 0)),
            pl.BlockSpec((1, n, 1, part, width), lambda k, o: (o[n + k], 0, 1, 0, 0)),
        ],
        out_specs=pl.BlockSpec((rows, width), lambda k, o: (0, 0)),
    )
    return pl.pallas_call(
        base_kernel,
        grid_spec=grid_spec,
        out_shape=jax.ShapeDtypeStruct((rows, width), F32),
        name="base",
        compiler_params=pltpu.CompilerParams(vmem_limit_bytes=10 << 20),
        cost_estimate=pl.CostEstimate(
            flops=2 * rows * matrix.size,
            bytes_accessed=2 * matrix.size + 2 * a_all.size + 2 * b_all.size + 4 * rows * width,
            transcendentals=0,
        ),
    )(order, a_all, b_all, weights, weights)


def down_kernel(order, hidden_ref, w_ref, *outs):
    n = len(outs) // 2
    half, span = outs[0].shape
    share = span // n
    step = pl.program_id(0)
    starts = [pl.multiple_of(order[n + m] * share, share) for m in range(n)]
    weights = jnp.concatenate([w_ref[:, pl.ds(start, share)] for start in starts], 1)
    product = dot_bf(hidden_ref[...], weights)
    for m in range(n):
        place = pl.ds(pl.multiple_of(step * share, share), share)
        outs[n + m][:, place] = product[half:, m * share : (m + 1) * share]
    for k in range(n):

        @pl.when(step == k)
        def _(k=k):
            outs[k][...] = product[:half]


def down_product(hidden, matrix, n):
    rows, depth = hidden.shape
    span = matrix.shape[1] // n
    order = jnp.concatenate([index_order("x", 1), index_order("y", 1)])
    grid_spec = pltpu.PrefetchScalarGridSpec(
        num_scalar_prefetch=1,
        grid=(n,),
        in_specs=[
            pl.BlockSpec((rows, depth), lambda k, o: (0, 0)),
            pl.BlockSpec((depth, span), lambda k, o: (0, o[k])),
        ],
        out_specs=[pl.BlockSpec((rows // 2, span), lambda k, o: (0, 0))] * (2 * n),
    )
    outs = pl.pallas_call(
        down_kernel,
        grid_spec=grid_spec,
        out_shape=[jax.ShapeDtypeStruct((rows // 2, span), BF)] * (2 * n),
        name="partial",
        compiler_params=pltpu.CompilerParams(vmem_limit_bytes=10 << 20),
        cost_estimate=pl.CostEstimate(
            flops=2 * rows * matrix.size,
            bytes_accessed=2 * matrix.size + 2 * hidden.size + 2 * rows * matrix.shape[1],
            transcendentals=0,
        ),
    )(order, hidden, matrix)
    return outs[:n], outs[n:]


def scatter_over(parts, axis):
    got = [shift(part, axis, step).astype(F32) for part, step in zip(parts[1:], (1, -1, 2))]
    return (parts[0].astype(F32) + got[0]) + (got[1] + got[2])


def scatter_sum(parts):
    low, high = parts
    n = len(low)
    low = scatter_over(low, "x").astype(BF)
    high = scatter_over(high, "y").astype(BF)
    low = scatter_over(jnp.split(low, n, 1), "y")
    high = scatter_over(jnp.split(high, n, 1), "x")
    return jnp.concatenate([low, high], 0)


def fan_out(start, depth, rank, slots):
    lane = lax.broadcasted_iota(jnp.int32, (depth, slots * rank), 1)
    row = lax.broadcasted_iota(jnp.int32, (depth, slots * rank), 0)
    return (row == lax.rem(lane, rank) + start).astype(BF)


def slot_mask(local, rows, rank, first, slots):
    lane = lax.broadcasted_iota(jnp.int32, (rows, slots * rank), 1) // rank + first
    return local.astype(F32).astype(jnp.int32) == lane


def split_rows(values, own_ref, other_ref, i):
    half = values.shape[0] // 2
    rows = pl.ds(i * half, half)
    return (own_ref, rows, values[:half]), (other_ref, rows, values[half:])


def in_rank_kernel(count, rank, *refs):
    tokens_ref, local_ref = refs[:2]
    factors = refs[2 : 2 + count]
    own_ref, other_ref = refs[2 + count :]
    slots = factors[0].shape[0]
    rows = tokens_ref.shape[1]
    for i in range(count):
        local = jnp.broadcast_to(local_ref[i].astype(F32), (rows, 2 * rank))

        def step(e, total, i=i, local=local):
            part = dot(tokens_ref[i], factors[i][e])
            return total + jnp.where(local == e.astype(F32), part, 0.0)

        total = lax.fori_loop(0, slots, step, jnp.zeros((rows, 2 * rank), F32), unroll=2)
        for ref, at, part in split_rows(total.astype(BF), own_ref, other_ref, i):
            ref[at, :] = part


def delta_kernel(count, rank, *refs):
    ranks_ref, local_ref = refs[:2]
    factors = refs[2 : 2 + 2 * count]
    own_ref, other_ref = refs[2 + 2 * count :]
    slots = factors[0].shape[0]
    width = factors[0].shape[2]
    rows = ranks_ref.shape[1]
    for which in range(2):
        fan = fan_out(which * rank, ranks_ref.shape[2], rank, slots)
        for i in range(count):
            wide = dot(ranks_ref[i], fan)
            wide = jnp.where(slot_mask(local_ref[i], rows, rank, 0, slots), wide, 0.0).astype(BF)
            delta = dot_bf(wide, factors[2 * i + which][...].reshape(slots * rank, width))
            for ref, at, part in split_rows(delta, own_ref, other_ref, i):
                ref[at, which * width : (which + 1) * width] = part


def down_rank_kernel(count, rank, *refs):
    hidden_ref, local_ref = refs[:2]
    factors = refs[2 : 2 + 2 * count]
    own_ref, other_ref = refs[2 + 2 * count :]
    slots = factors[0].shape[0]
    rows, depth = hidden_ref.shape[1:]
    fan = fan_out(0, rank, rank, slots)
    for i in range(count):
        total = jnp.zeros((rows, rank), F32)
        for which in range(2):
            factor = factors[2 * i + which][:, :, :depth].reshape(slots * rank, depth)
            part = lax.dot_general(
                hidden_ref[i], factor, (((1,), (1,)), ((), ())), preferred_element_type=F32
            )
            mask = slot_mask(local_ref[i], rows, rank, which * slots, slots)
            part = jnp.where(mask, part, 0.0).astype(BF)
            total += lax.dot_general(part, fan, (((1,), (1,)), ((), ())), preferred_element_type=F32)
        for ref, at, part in split_rows(total.astype(BF), own_ref, other_ref, i):
            ref[at, :] = part


def down_delta_kernel(count, rank, *refs):
    ranks_ref, local_ref = refs[:2]
    factors = refs[2 : 2 + 2 * count]
    own_ref, other_ref = refs[2 + 2 * count :]
    slots = factors[0].shape[0]
    rows = ranks_ref.shape[1]
    width = own_ref.shape[1]
    fan = fan_out(0, rank, rank, slots)
    for i in range(count):
        total = jnp.zeros((rows, width), F32)
        spread = dot(ranks_ref[i], fan)
        for which in range(2):
            mask = slot_mask(local_ref[i], rows, rank, which * slots, slots)
            wide = jnp.where(mask, spread, 0.0).astype(BF)
            factor = factors[2 * i + which]
            factor = factor[:, :, factor.shape[2] - width :].reshape(slots * rank, width)
            total += dot(wide, factor)
        for ref, at, part in split_rows(total.astype(BF), own_ref, other_ref, i):
            ref[at, :] = part


def seated_call(kernel, rank, seated, local, factors, width, flops):
    count, rows = seated.shape[:2]
    out = jax.ShapeDtypeStruct((count * rows // 2, width), BF)
    flat = [f for pair in factors for f in pair]
    moved = sum(2 * f.size for f in flat) + 4 * out.size + 2 * seated.size
    return pl.pallas_call(
        functools.partial(kernel, count, rank),
        in_specs=[pl.BlockSpec(memory_space=pltpu.VMEM)] * (2 + len(flat)),
        out_specs=[pl.BlockSpec(memory_space=pltpu.VMEM)] * 2,
        out_shape=[out, out],
        compiler_params=pltpu.CompilerParams(vmem_limit_bytes=9 << 20),
        cost_estimate=pl.CostEstimate(flops=flops, bytes_accessed=moved, transcendentals=0),
    )(seated, local, *flat)


def layer(
    tokens,
    token_tenant,
    tenant_storage_slot,
    gate_matrix,
    up_matrix,
    down_matrix,
    adapter_gate_up_inputs,
    adapter_gate_up_outputs,
    adapter_down_inputs,
    adapter_down_outputs,
):
    groups = lax.axis_size(GRP)
    rows = tokens.shape[0]
    block_slots = adapter_gate_up_inputs.shape[0]
    rank = adapter_gate_up_inputs.shape[2] // 2
    hidden_share = gate_matrix.shape[1]
    width_share = tokens.shape[1]
    capacity = 2 * rows // groups
    chips = groups // 2
    side = chips * capacity

    in_factors = [(adapter_gate_up_inputs,)]
    in_factors += [(shift(adapter_gate_up_inputs, "z", step),) for step in (1, -1, 2)]
    pieces = gather_tokens(tokens)
    gate_part = adapter_gate_up_outputs[:, :rank, :]
    up_part = adapter_gate_up_outputs[:, rank:, :]
    out_factors = ring(gate_part, up_part)
    down_in = adapter_down_inputs.swapaxes(1, 2)
    half = block_slots // 2
    low = jnp.concatenate([down_in[:half], adapter_down_outputs[:half]], 2)
    high = jnp.concatenate([down_in[half:], adapter_down_outputs[half:]], 2)
    down_factors = ring(low, high)
    base_gate = base_product(pieces, gate_matrix)
    base_up = base_product(pieces, up_matrix)

    tokens_pair = (tokens, swap(tokens))
    tenants = jnp.stack([token_tenant, swap(token_tenant)])
    table = jnp.arange(tenant_storage_slot.shape[0], dtype=jnp.int32)
    match = tenants[:, :, None] == table[None, None, :]
    slot = jnp.sum(jnp.where(match, tenant_storage_slot[None, None, :], 0), 2)
    server = slot // block_slots
    local = slot - server * block_slots
    picks = (server[:, :, None] == jnp.arange(groups, dtype=jnp.int32)).astype(jnp.int32)
    place = jnp.sum(picks * (jnp.cumsum(picks, 1) - 1), 2)
    apart = lax.rem(server // 2 - lax.axis_index("z") + chips, chips)
    turn = jnp.where(apart == 0, 0, jnp.where(apart == chips - 1, 1, jnp.where(apart == 1, 2, 3)))
    seat = turn * capacity + place
    mine = lax.rem(server, 2) == lax.axis_index("c")
    here = jnp.where(mine, seat, -1)
    there = jnp.where(mine, -1, seat)[0]
    seats = jnp.arange(side, dtype=jnp.int32)
    take = (seats[None, :, None] == here[:, None, :]).astype(BF)
    give_here = (here[0][:, None] == seats[None, :]).astype(BF)
    give_there = (there[:, None] == seats[None, :]).astype(BF)

    def by_block(pair):
        packed = [dot_bf(take[g], v).reshape(chips, capacity, -1) for g, v in enumerate(pair)]
        return jnp.concatenate(packed, 1)

    def home(own, other):
        return dot(give_here, own) + dot(give_there, other)

    seat_local = by_block((local[0][:, None].astype(BF), local[1][:, None].astype(BF)))

    seated = by_block(tokens_pair)
    flops = 8 * side * block_slots * rank * width_share
    own, other = seated_call(in_rank_kernel, rank, seated, seat_local, in_factors, 2 * rank, flops)
    home_part = home(own, swap(other)).astype(BF)
    ranks = sum_tp(home_part)
    seated_ranks = by_block((ranks, swap(ranks)))

    flops = 8 * side * block_slots * rank * hidden_share
    own, other = seated_call(
        delta_kernel, rank, seated_ranks, seat_local, out_factors, 2 * hidden_share, flops
    )
    other = swap(other)
    gate = base_gate + home(own[:, :hidden_share], other[:, :hidden_share])
    up = base_up + home(own[:, hidden_share:], other[:, hidden_share:])
    hidden = (jax.nn.silu(gate) * up).astype(BF)

    partial = down_product(hidden, down_matrix, lax.axis_size("x"))
    hidden_pair = (hidden, swap(hidden))
    summed = scatter_sum(partial)

    seated_hidden = by_block(hidden_pair)
    flops = 4 * side * block_slots * rank * hidden_share
    own, other = seated_call(
        down_rank_kernel, rank, seated_hidden, seat_local, down_factors, rank, flops
    )
    down_rows = home(own, swap(other)).astype(BF)
    down_ranks = sum_tp(down_rows)
    seated_down = by_block((down_ranks, swap(down_ranks)))
    flops = 4 * side * block_slots * rank * width_share
    own, other = seated_call(
        down_delta_kernel, rank, seated_down, seat_local, down_factors, width_share, flops
    )
    returned = home(own, swap(other))
    return (summed + returned).astype(BF)


def solution(mesh):
    sizes = mesh.devices.shape
    cores = 2
    side = 4
    fine = Mesh(
        mesh.devices.reshape(sizes[0] // cores, cores, sizes[1] // side, side),
        ("z", "c", "x", "y"),
    )
    return jax.shard_map(
        layer,
        mesh=fine,
        in_specs=(
            P(GRP, TP),
            P(GRP),
            P(),
            P(None, TP),
            P(None, TP),
            P(TP, None),
            P(GRP, TP, None),
            P(GRP, None, TP),
            P(GRP, TP, None),
            P(GRP, None, TP),
        ),
        out_specs=P(GRP, TP),
        check_vma=False,
    )
```

```python
import functools

import jax
import jax.numpy as jnp
from jax import lax
from jax.experimental import pallas as pl
from jax.experimental.pallas import tpu as pltpu
from jax.sharding import Mesh, PartitionSpec as P

GRP = ("z", "c")
TP = ("x", "y")
BF = jnp.bfloat16
F32 = jnp.float32


def dot(a, b):
    return jnp.dot(a, b, preferred_element_type=F32)


def dot_bf(a, b):
    return dot(a, b).astype(BF)


def shift(values, axis, step):
    n = lax.axis_size(axis)
    return lax.ppermute(values, axis, [(i, (i + step) % n) for i in range(n)])


def swap(values):
    return shift(values, "c", 1)


def sum_over(values, axis):
    got = [shift(values, axis, step).astype(F32) for step in (1, -1, 2)]
    return ((values.astype(F32) + got[0]) + (got[1] + got[2])).astype(BF)


def sum_tp(values):
    first = sum_over(values, "x")
    return sum_over(first, "y")


def ring(first, second):
    below = (shift(first, "z", 1), shift(second, "z", 1))
    above = (shift(first, "z", -1), shift(second, "z", -1))
    far = (shift(below[0], "z", 1), shift(above[1], "z", -1))
    return [(first, second), below, above, far]


def base_kernel(order, a_ref, b_ref, wa_ref, wb_ref, out_ref):
    n, _, part = a_ref.shape[1:]
    pieces = [a_ref[0, order[2 * n + i]] for i in range(n)]
    pieces += [b_ref[0, order[3 * n + i]] for i in range(n)]
    width = wa_ref.shape[-1]
    wa = wa_ref[...].reshape(n * part, width)
    wb = wb_ref[...].reshape(n * part, width)
    product = dot(jnp.concatenate(pieces, 1), jnp.concatenate([wa, wb], 0))
    first = pl.program_id(0) == 0

    @pl.when(first)
    def _():
        out_ref[...] = product

    @pl.when(jnp.logical_not(first))
    def _():
        out_ref[...] += product


def peers(values, axis):
    return jnp.stack([values] + [shift(values, axis, step) for step in (1, -1, 2)])


def index_order(axis, sign):
    n = lax.axis_size(axis)
    which = jnp.arange(n, dtype=jnp.int32)
    step = jnp.where(which == 0, 0, jnp.where(which == 1, 1, jnp.where(which == 2, -1, 2)))
    return lax.rem(lax.axis_index(axis) + sign * step + n, n).astype(jnp.int32)


def place_order(axis):
    n = lax.axis_size(axis)
    apart = lax.rem(lax.axis_index(axis) - jnp.arange(n, dtype=jnp.int32) + n, n)
    return jnp.where(apart == 0, 0, jnp.where(apart == 1, 1, jnp.where(apart == n - 1, 2, 3)))


def gather_tokens(tokens):
    part = tokens.shape[1] // 2
    a_line = peers(tokens[:, :part], "x")
    b_line = peers(tokens[:, part:], "y")
    return peers(a_line, "y"), peers(b_line, "x")


def base_product(pieces, matrix):
    a_all, b_all = pieces
    n, _, rows, part = a_all.shape
    width = matrix.shape[1]
    order = jnp.concatenate(
        [index_order("y", -1), index_order("x", -1), place_order("x"), place_order("y")]
    )
    weights = matrix.reshape(n, n, 2, part, width)
    line = pl.BlockSpec((1, n, rows, part), lambda k, o: (k, 0, 0, 0))
    grid_spec = pltpu.PrefetchScalarGridSpec(
        num_scalar_prefetch=1,
        grid=(n,),
        in_specs=[
            line,
            line,
            pl.BlockSpec((n, 1, 1, part, width), lambda k, o: (0, o[k], 0, 0, 0)),
            pl.BlockSpec((1, n, 1, part, width), lambda k, o: (o[n + k], 0, 1, 0, 0)),
        ],
        out_specs=pl.BlockSpec((rows, width), lambda k, o: (0, 0)),
    )
    return pl.pallas_call(
        base_kernel,
        grid_spec=grid_spec,
        out_shape=jax.ShapeDtypeStruct((rows, width), F32),
        name="base",
        compiler_params=pltpu.CompilerParams(vmem_limit_bytes=10 << 20),
        cost_estimate=pl.CostEstimate(
            flops=2 * rows * matrix.size,
            bytes_accessed=2 * matrix.size + 2 * a_all.size + 2 * b_all.size + 4 * rows * width,
            transcendentals=0,
        ),
    )(order, a_all, b_all, weights, weights)


def hidden_kernel(here_ref, there_ref, own_ref, other_ref, gate_ref, up_ref, out_ref):
    width = out_ref.shape[1]
    delta = dot(here_ref[...], own_ref[...]) + dot(there_ref[...], other_ref[...])
    gate = gate_ref[...] + delta[:, :width]
    up = up_ref[...] + delta[:, width:]
    out_ref[...] = (gate / (1.0 + jnp.exp(-gate)) * up).astype(BF)


def hidden_rows(here, there, own, other, base_gate, base_up):
    rows, width = base_gate.shape
    seats = here.shape[1]
    block = rows // 4
    row_block = pl.BlockSpec((block, width), lambda k: (k, 0))
    seat_block = pl.BlockSpec((block, seats), lambda k: (k, 0))
    whole = pl.BlockSpec((seats, 2 * width), lambda k: (0, 0))
    return pl.pallas_call(
        hidden_kernel,
        grid=(rows // block,),
        in_specs=[seat_block, seat_block, whole, whole, row_block, row_block],
        out_specs=row_block,
        out_shape=jax.ShapeDtypeStruct((rows, width), BF),
        name="hidden",
        compiler_params=pltpu.CompilerParams(vmem_limit_bytes=14 << 20),
        cost_estimate=pl.CostEstimate(
            flops=8 * rows * seats * width,
            bytes_accessed=8 * seats * width + 10 * rows * width,
            transcendentals=rows * width,
        ),
    )(here, there, own, other, base_gate, base_up)


def down_kernel(order, hidden_ref, w_ref, *outs):
    n = len(outs) // 2
    half, span = outs[0].shape
    share = span // n
    step = pl.program_id(0)
    starts = [pl.multiple_of(order[n + m] * share, share) for m in range(n)]
    weights = jnp.concatenate([w_ref[:, pl.ds(start, share)] for start in starts], 1)
    product = dot_bf(hidden_ref[...], weights)
    for m in range(n):
        place = pl.ds(pl.multiple_of(step * share, share), share)
        outs[n + m][:, place] = product[half:, m * share : (m + 1) * share]
    for k in range(n):

        @pl.when(step == k)
        def _(k=k):
            outs[k][...] = product[:half]


def down_product(hidden, matrix, n):
    rows, depth = hidden.shape
    span = matrix.shape[1] // n
    order = jnp.concatenate([index_order("x", 1), index_order("y", 1)])
    grid_spec = pltpu.PrefetchScalarGridSpec(
        num_scalar_prefetch=1,
        grid=(n,),
        in_specs=[
            pl.BlockSpec((rows, depth), lambda k, o: (0, 0)),
            pl.BlockSpec((depth, span), lambda k, o: (0, o[k])),
        ],
        out_specs=[pl.BlockSpec((rows // 2, span), lambda k, o: (0, 0))] * (2 * n),
    )
    outs = pl.pallas_call(
        down_kernel,
        grid_spec=grid_spec,
        out_shape=[jax.ShapeDtypeStruct((rows // 2, span), BF)] * (2 * n),
        name="partial",
        compiler_params=pltpu.CompilerParams(vmem_limit_bytes=10 << 20),
        cost_estimate=pl.CostEstimate(
            flops=2 * rows * matrix.size,
            bytes_accessed=2 * matrix.size + 2 * hidden.size + 2 * rows * matrix.shape[1],
            transcendentals=0,
        ),
    )(order, hidden, matrix)
    return outs[:n], outs[n:]


def scatter_over(parts, axis):
    got = [shift(part, axis, step).astype(F32) for part, step in zip(parts[1:], (1, -1, 2))]
    return (parts[0].astype(F32) + got[0]) + (got[1] + got[2])


def scatter_sum(parts):
    low, high = parts
    n = len(low)
    low = scatter_over(low, "x").astype(BF)
    high = scatter_over(high, "y").astype(BF)
    low = scatter_over(jnp.split(low, n, 1), "y")
    high = scatter_over(jnp.split(high, n, 1), "x")
    return jnp.concatenate([low, high], 0)


def fan_out(start, depth, rank, slots):
    lane = lax.broadcasted_iota(jnp.int32, (depth, slots * rank), 1)
    row = lax.broadcasted_iota(jnp.int32, (depth, slots * rank), 0)
    return (row == lax.rem(lane, rank) + start).astype(BF)


def slot_mask(local, rows, rank, first, slots):
    lane = lax.broadcasted_iota(jnp.int32, (rows, slots * rank), 1) // rank + first
    return local.astype(F32).astype(jnp.int32) == lane


def split_rows(values, own_ref, other_ref, i):
    half = values.shape[0] // 2
    rows = pl.ds(i * half, half)
    return (own_ref, rows, values[:half]), (other_ref, rows, values[half:])


def in_rank_kernel(count, rank, *refs):
    tokens_ref, local_ref = refs[:2]
    factors = refs[2 : 2 + count]
    own_ref, other_ref = refs[2 + count :]
    slots = factors[0].shape[0]
    rows = tokens_ref.shape[1]
    for i in range(count):
        local = jnp.broadcast_to(local_ref[i].astype(F32), (rows, 2 * rank))

        def step(e, total, i=i, local=local):
            part = dot(tokens_ref[i], factors[i][e])
            return total + jnp.where(local == e.astype(F32), part, 0.0)

        total = lax.fori_loop(0, slots, step, jnp.zeros((rows, 2 * rank), F32), unroll=2)
        for ref, at, part in split_rows(total.astype(BF), own_ref, other_ref, i):
            ref[at, :] = part


def delta_kernel(count, rank, *refs):
    ranks_ref, local_ref = refs[:2]
    factors = refs[2 : 2 + 2 * count]
    own_ref, other_ref = refs[2 + 2 * count :]
    slots = factors[0].shape[0]
    width = factors[0].shape[2]
    rows = ranks_ref.shape[1]
    for which in range(2):
        fan = fan_out(which * rank, ranks_ref.shape[2], rank, slots)
        for i in range(count):
            wide = dot(ranks_ref[i], fan)
            wide = jnp.where(slot_mask(local_ref[i], rows, rank, 0, slots), wide, 0.0).astype(BF)
            delta = dot_bf(wide, factors[2 * i + which][...].reshape(slots * rank, width))
            for ref, at, part in split_rows(delta, own_ref, other_ref, i):
                ref[at, which * width : (which + 1) * width] = part


def down_rank_kernel(count, rank, *refs):
    hidden_ref, local_ref = refs[:2]
    factors = refs[2 : 2 + 2 * count]
    own_ref, other_ref = refs[2 + 2 * count :]
    slots = factors[0].shape[0]
    rows, depth = hidden_ref.shape[1:]
    fan = fan_out(0, rank, rank, slots)
    for i in range(count):
        total = jnp.zeros((rows, rank), F32)
        for which in range(2):
            factor = factors[2 * i + which][:, :, :depth].reshape(slots * rank, depth)
            part = lax.dot_general(
                hidden_ref[i], factor, (((1,), (1,)), ((), ())), preferred_element_type=F32
            )
            mask = slot_mask(local_ref[i], rows, rank, which * slots, slots)
            part = jnp.where(mask, part, 0.0).astype(BF)
            total += lax.dot_general(part, fan, (((1,), (1,)), ((), ())), preferred_element_type=F32)
        for ref, at, part in split_rows(total.astype(BF), own_ref, other_ref, i):
            ref[at, :] = part


def down_delta_kernel(count, rank, *refs):
    ranks_ref, local_ref = refs[:2]
    factors = refs[2 : 2 + 2 * count]
    own_ref, other_ref = refs[2 + 2 * count :]
    slots = factors[0].shape[0]
    rows = ranks_ref.shape[1]
    width = own_ref.shape[1]
    fan = fan_out(0, rank, rank, slots)
    for i in range(count):
        total = jnp.zeros((rows, width), F32)
        spread = dot(ranks_ref[i], fan)
        for which in range(2):
            mask = slot_mask(local_ref[i], rows, rank, which * slots, slots)
            wide = jnp.where(mask, spread, 0.0).astype(BF)
            factor = factors[2 * i + which]
            factor = factor[:, :, factor.shape[2] - width :].reshape(slots * rank, width)
            total += dot(wide, factor)
        for ref, at, part in split_rows(total.astype(BF), own_ref, other_ref, i):
            ref[at, :] = part


def seated_call(kernel, rank, seated, local, factors, width, flops):
    count, rows = seated.shape[:2]
    out = jax.ShapeDtypeStruct((count * rows // 2, width), BF)
    flat = [f for pair in factors for f in pair]
    moved = sum(2 * f.size for f in flat) + 4 * out.size + 2 * seated.size
    return pl.pallas_call(
        functools.partial(kernel, count, rank),
        in_specs=[pl.BlockSpec(memory_space=pltpu.VMEM)] * (2 + len(flat)),
        out_specs=[pl.BlockSpec(memory_space=pltpu.VMEM)] * 2,
        out_shape=[out, out],
        compiler_params=pltpu.CompilerParams(vmem_limit_bytes=9 << 20),
        cost_estimate=pl.CostEstimate(flops=flops, bytes_accessed=moved, transcendentals=0),
    )(seated, local, *flat)


def layer(
    tokens,
    token_tenant,
    tenant_storage_slot,
    gate_matrix,
    up_matrix,
    down_matrix,
    adapter_gate_up_inputs,
    adapter_gate_up_outputs,
    adapter_down_inputs,
    adapter_down_outputs,
):
    groups = lax.axis_size(GRP)
    rows = tokens.shape[0]
    block_slots = adapter_gate_up_inputs.shape[0]
    rank = adapter_gate_up_inputs.shape[2] // 2
    hidden_share = gate_matrix.shape[1]
    width_share = tokens.shape[1]
    capacity = 2 * rows // groups
    chips = groups // 2
    side = chips * capacity

    in_factors = [(adapter_gate_up_inputs,)]
    in_factors += [(shift(adapter_gate_up_inputs, "z", step),) for step in (1, -1, 2)]
    pieces = gather_tokens(tokens)
    gate_part = adapter_gate_up_outputs[:, :rank, :]
    up_part = adapter_gate_up_outputs[:, rank:, :]
    out_factors = ring(gate_part, up_part)
    down_in = adapter_down_inputs.swapaxes(1, 2)
    half = block_slots // 2
    low = jnp.concatenate([down_in[:half], adapter_down_outputs[:half]], 2)
    high = jnp.concatenate([down_in[half:], adapter_down_outputs[half:]], 2)
    down_factors = ring(low, high)
    base_gate = base_product(pieces, gate_matrix)
    base_up = base_product(pieces, up_matrix)

    tokens_pair = (tokens, swap(tokens))
    tenants = jnp.stack([token_tenant, swap(token_tenant)])
    table = jnp.arange(tenant_storage_slot.shape[0], dtype=jnp.int32)
    match = tenants[:, :, None] == table[None, None, :]
    slot = jnp.sum(jnp.where(match, tenant_storage_slot[None, None, :], 0), 2)
    server = slot // block_slots
    local = slot - server * block_slots
    picks = (server[:, :, None] == jnp.arange(groups, dtype=jnp.int32)).astype(jnp.int32)
    place = jnp.sum(picks * (jnp.cumsum(picks, 1) - 1), 2)
    apart = lax.rem(server // 2 - lax.axis_index("z") + chips, chips)
    turn = jnp.where(apart == 0, 0, jnp.where(apart == chips - 1, 1, jnp.where(apart == 1, 2, 3)))
    seat = turn * capacity + place
    mine = lax.rem(server, 2) == lax.axis_index("c")
    here = jnp.where(mine, seat, -1)
    there = jnp.where(mine, -1, seat)[0]
    seats = jnp.arange(side, dtype=jnp.int32)
    take = (seats[None, :, None] == here[:, None, :]).astype(BF)
    give_here = (here[0][:, None] == seats[None, :]).astype(BF)
    give_there = (there[:, None] == seats[None, :]).astype(BF)

    def by_block(pair):
        packed = [dot_bf(take[g], v).reshape(chips, capacity, -1) for g, v in enumerate(pair)]
        return jnp.concatenate(packed, 1)

    def home(own, other):
        return dot(give_here, own) + dot(give_there, other)

    seat_local = by_block((local[0][:, None].astype(BF), local[1][:, None].astype(BF)))

    seated = by_block(tokens_pair)
    flops = 8 * side * block_slots * rank * width_share
    own, other = seated_call(in_rank_kernel, rank, seated, seat_local, in_factors, 2 * rank, flops)
    home_part = home(own, swap(other)).astype(BF)
    ranks = sum_tp(home_part)
    seated_ranks = by_block((ranks, swap(ranks)))

    flops = 8 * side * block_slots * rank * hidden_share
    own, other = seated_call(
        delta_kernel, rank, seated_ranks, seat_local, out_factors, 2 * hidden_share, flops
    )
    other = swap(other)
    hidden = hidden_rows(give_here, give_there, own, other, base_gate, base_up)

    partial = down_product(hidden, down_matrix, lax.axis_size("x"))
    hidden_pair = (hidden, swap(hidden))
    summed = scatter_sum(partial)

    seated_hidden = by_block(hidden_pair)
    flops = 4 * side * block_slots * rank * hidden_share
    own, other = seated_call(
        down_rank_kernel, rank, seated_hidden, seat_local, down_factors, rank, flops
    )
    down_rows = home(own, swap(other)).astype(BF)
    down_ranks = sum_tp(down_rows)
    seated_down = by_block((down_ranks, swap(down_ranks)))
    flops = 4 * side * block_slots * rank * width_share
    own, other = seated_call(
        down_delta_kernel, rank, seated_down, seat_local, down_factors, width_share, flops
    )
    returned = home(own, swap(other))
    return (summed + returned).astype(BF)


def solution(mesh):
    sizes = mesh.devices.shape
    cores = 2
    side = 4
    fine = Mesh(
        mesh.devices.reshape(sizes[0] // cores, cores, sizes[1] // side, side),
        ("z", "c", "x", "y"),
    )
    return jax.shard_map(
        layer,
        mesh=fine,
        in_specs=(
            P(GRP, TP),
            P(GRP),
            P(),
            P(None, TP),
            P(None, TP),
            P(TP, None),
            P(GRP, TP, None),
            P(GRP, None, TP),
            P(GRP, TP, None),
            P(GRP, None, TP),
        ),
        out_specs=P(GRP, TP),
        check_vma=False,
    )
```

```python
import functools

import jax
import jax.numpy as jnp
from jax import lax
from jax.experimental import pallas as pl
from jax.experimental.pallas import tpu as pltpu
from jax.sharding import Mesh, PartitionSpec as P

GRP = ("z", "c")
TP = ("x", "y")
BF = jnp.bfloat16
F32 = jnp.float32


def dot(a, b):
    return jnp.dot(a, b, preferred_element_type=F32)


def dot_bf(a, b):
    return dot(a, b).astype(BF)


def shift(values, axis, step):
    n = lax.axis_size(axis)
    return lax.ppermute(values, axis, [(i, (i + step) % n) for i in range(n)])


def swap(values):
    return shift(values, "c", 1)


def sum_over(values, axis):
    got = [shift(values, axis, step).astype(F32) for step in (1, -1, 2)]
    return ((values.astype(F32) + got[0]) + (got[1] + got[2])).astype(BF)


def sum_tp(values):
    first = sum_over(values, "x")
    return sum_over(first, "y")


def ring(first, second):
    below = (shift(first, "z", 1), shift(second, "z", 1))
    above = (shift(first, "z", -1), shift(second, "z", -1))
    far = (shift(below[0], "z", 1), shift(above[1], "z", -1))
    return [(first, second), below, above, far]


def base_kernel(order, a_ref, b_ref, wa_ref, wb_ref, out_ref):
    n, rows, part = a_ref.shape[1:]
    width = wa_ref.shape[-1]
    wa = wa_ref[...].reshape(n * part, width)
    wb = wb_ref[...].reshape(n * part, width)
    weights = jnp.concatenate([wa, wb], 0)
    block = rows // 2

    @pl.when(pl.program_id(0) == 0)
    def _():
        out_ref[...] = jnp.zeros_like(out_ref)

    def tile(t, carry):
        at = pl.ds(pl.multiple_of(t * block, block), block)
        left = [a_ref[0, order[2 * n + i], at, :] for i in range(n)]
        left += [b_ref[0, order[3 * n + i], at, :] for i in range(n)]
        out_ref[at, :] += dot(jnp.concatenate(left, 1), weights)
        return carry

    lax.fori_loop(0, 2, tile, 0)


def peers(values, axis):
    return jnp.stack([values] + [shift(values, axis, step) for step in (1, -1, 2)])


def index_order(axis, sign):
    n = lax.axis_size(axis)
    which = jnp.arange(n, dtype=jnp.int32)
    step = jnp.where(which == 0, 0, jnp.where(which == 1, 1, jnp.where(which == 2, -1, 2)))
    return lax.rem(lax.axis_index(axis) + sign * step + n, n).astype(jnp.int32)


def place_order(axis):
    n = lax.axis_size(axis)
    apart = lax.rem(lax.axis_index(axis) - jnp.arange(n, dtype=jnp.int32) + n, n)
    return jnp.where(apart == 0, 0, jnp.where(apart == 1, 1, jnp.where(apart == n - 1, 2, 3)))


def gather_tokens(tokens):
    part = tokens.shape[1] // 2
    a_line = peers(tokens[:, :part], "x")
    b_line = peers(tokens[:, part:], "y")
    return peers(a_line, "y"), peers(b_line, "x")


def base_product(pieces, matrix):
    a_all, b_all = pieces
    n, _, rows, part = a_all.shape
    width = matrix.shape[1]
    order = jnp.concatenate(
        [index_order("y", -1), index_order("x", -1), place_order("x"), place_order("y")]
    )
    weights = matrix.reshape(n, n, 2, part, width)
    line = pl.BlockSpec((1, n, rows, part), lambda k, o: (k, 0, 0, 0))
    grid_spec = pltpu.PrefetchScalarGridSpec(
        num_scalar_prefetch=1,
        grid=(n,),
        in_specs=[
            line,
            line,
            pl.BlockSpec((n, 1, 1, part, width), lambda k, o: (0, o[k], 0, 0, 0)),
            pl.BlockSpec((1, n, 1, part, width), lambda k, o: (o[n + k], 0, 1, 0, 0)),
        ],
        out_specs=pl.BlockSpec((rows, width), lambda k, o: (0, 0)),
    )
    return pl.pallas_call(
        base_kernel,
        grid_spec=grid_spec,
        out_shape=jax.ShapeDtypeStruct((rows, width), F32),
        name="base",
        compiler_params=pltpu.CompilerParams(vmem_limit_bytes=10 << 20),
        cost_estimate=pl.CostEstimate(
            flops=2 * rows * matrix.size,
            bytes_accessed=2 * matrix.size + 2 * a_all.size + 2 * b_all.size + 4 * rows * width,
            transcendentals=0,
        ),
    )(order, a_all, b_all, weights, weights)


def hidden_kernel(here_ref, there_ref, own_ref, other_ref, gate_ref, up_ref, out_ref):
    width = out_ref.shape[1]
    delta = dot(here_ref[...], own_ref[...]) + dot(there_ref[...], other_ref[...])
    gate = gate_ref[...] + delta[:, :width]
    up = up_ref[...] + delta[:, width:]
    out_ref[...] = (gate / (1.0 + jnp.exp(-gate)) * up).astype(BF)


def hidden_rows(here, there, own, other, base_gate, base_up):
    rows, width = base_gate.shape
    seats = here.shape[1]
    block = rows // 4
    row_block = pl.BlockSpec((block, width), lambda k: (k, 0))
    seat_block = pl.BlockSpec((block, seats), lambda k: (k, 0))
    whole = pl.BlockSpec((seats, 2 * width), lambda k: (0, 0))
    return pl.pallas_call(
        hidden_kernel,
        grid=(rows // block,),
        in_specs=[seat_block, seat_block, whole, whole, row_block, row_block],
        out_specs=row_block,
        out_shape=jax.ShapeDtypeStruct((rows, width), BF),
        name="hidden",
        compiler_params=pltpu.CompilerParams(vmem_limit_bytes=14 << 20),
        cost_estimate=pl.CostEstimate(
            flops=8 * rows * seats * width,
            bytes_accessed=8 * seats * width + 10 * rows * width,
            transcendentals=rows * width,
        ),
    )(here, there, own, other, base_gate, base_up)


def down_kernel(order, hidden_ref, w_ref, *outs):
    n = len(outs) // 2
    half, span = outs[0].shape
    share = span // n
    step = pl.program_id(0)
    starts = [pl.multiple_of(order[n + m] * share, share) for m in range(n)]
    weights = jnp.concatenate([w_ref[:, pl.ds(start, share)] for start in starts], 1)
    product = dot_bf(hidden_ref[...], weights)
    for m in range(n):
        place = pl.ds(pl.multiple_of(step * share, share), share)
        outs[n + m][:, place] = product[half:, m * share : (m + 1) * share]
    for k in range(n):

        @pl.when(step == k)
        def _(k=k):
            outs[k][...] = product[:half]


def down_product(hidden, matrix, n):
    rows, depth = hidden.shape
    span = matrix.shape[1] // n
    order = jnp.concatenate([index_order("x", 1), index_order("y", 1)])
    grid_spec = pltpu.PrefetchScalarGridSpec(
        num_scalar_prefetch=1,
        grid=(n,),
        in_specs=[
            pl.BlockSpec((rows, depth), lambda k, o: (0, 0)),
            pl.BlockSpec((depth, span), lambda k, o: (0, o[k])),
        ],
        out_specs=[pl.BlockSpec((rows // 2, span), lambda k, o: (0, 0))] * (2 * n),
    )
    outs = pl.pallas_call(
        down_kernel,
        grid_spec=grid_spec,
        out_shape=[jax.ShapeDtypeStruct((rows // 2, span), BF)] * (2 * n),
        name="partial",
        compiler_params=pltpu.CompilerParams(vmem_limit_bytes=10 << 20),
        cost_estimate=pl.CostEstimate(
            flops=2 * rows * matrix.size,
            bytes_accessed=2 * matrix.size + 2 * hidden.size + 2 * rows * matrix.shape[1],
            transcendentals=0,
        ),
    )(order, hidden, matrix)
    return outs[:n], outs[n:]


def scatter_over(parts, axis):
    got = [shift(part, axis, step).astype(F32) for part, step in zip(parts[1:], (1, -1, 2))]
    return (parts[0].astype(F32) + got[0]) + (got[1] + got[2])


def scatter_sum(parts):
    low, high = parts
    n = len(low)
    low = scatter_over(low, "x").astype(BF)
    high = scatter_over(high, "y").astype(BF)
    low = scatter_over(jnp.split(low, n, 1), "y")
    high = scatter_over(jnp.split(high, n, 1), "x")
    return jnp.concatenate([low, high], 0)


def fan_out(start, depth, rank, slots):
    lane = lax.broadcasted_iota(jnp.int32, (depth, slots * rank), 1)
    row = lax.broadcasted_iota(jnp.int32, (depth, slots * rank), 0)
    return (row == lax.rem(lane, rank) + start).astype(BF)


def slot_mask(local, rows, rank, first, slots):
    lane = lax.broadcasted_iota(jnp.int32, (rows, slots * rank), 1) // rank + first
    return local.astype(F32).astype(jnp.int32) == lane


def split_rows(values, own_ref, other_ref, i):
    half = values.shape[0] // 2
    rows = pl.ds(i * half, half)
    return (own_ref, rows, values[:half]), (other_ref, rows, values[half:])


def in_rank_kernel(count, rank, *refs):
    tokens_ref, local_ref = refs[:2]
    factors = refs[2 : 2 + count]
    own_ref, other_ref = refs[2 + count :]
    slots = factors[0].shape[0]
    rows = tokens_ref.shape[1]
    for i in range(count):
        local = jnp.broadcast_to(local_ref[i].astype(F32), (rows, 2 * rank))

        def step(e, total, i=i, local=local):
            part = dot(tokens_ref[i], factors[i][e])
            return total + jnp.where(local == e.astype(F32), part, 0.0)

        total = lax.fori_loop(0, slots, step, jnp.zeros((rows, 2 * rank), F32), unroll=2)
        for ref, at, part in split_rows(total.astype(BF), own_ref, other_ref, i):
            ref[at, :] = part


def delta_kernel(count, rank, *refs):
    ranks_ref, local_ref = refs[:2]
    factors = refs[2 : 2 + 2 * count]
    own_ref, other_ref = refs[2 + 2 * count :]
    slots = factors[0].shape[0]
    width = factors[0].shape[2]
    rows = ranks_ref.shape[1]
    for which in range(2):
        fan = fan_out(which * rank, ranks_ref.shape[2], rank, slots)
        for i in range(count):
            wide = dot(ranks_ref[i], fan)
            wide = jnp.where(slot_mask(local_ref[i], rows, rank, 0, slots), wide, 0.0).astype(BF)
            delta = dot_bf(wide, factors[2 * i + which][...].reshape(slots * rank, width))
            for ref, at, part in split_rows(delta, own_ref, other_ref, i):
                ref[at, which * width : (which + 1) * width] = part


def down_rank_kernel(count, rank, *refs):
    hidden_ref, local_ref = refs[:2]
    factors = refs[2 : 2 + 2 * count]
    own_ref, other_ref = refs[2 + 2 * count :]
    slots = factors[0].shape[0]
    rows, depth = hidden_ref.shape[1:]
    fan = fan_out(0, rank, rank, slots)
    for i in range(count):
        total = jnp.zeros((rows, rank), F32)
        for which in range(2):
            factor = factors[2 * i + which][:, :, :depth].reshape(slots * rank, depth)
            part = lax.dot_general(
                hidden_ref[i], factor, (((1,), (1,)), ((), ())), preferred_element_type=F32
            )
            mask = slot_mask(local_ref[i], rows, rank, which * slots, slots)
            part = jnp.where(mask, part, 0.0).astype(BF)
            total += lax.dot_general(part, fan, (((1,), (1,)), ((), ())), preferred_element_type=F32)
        for ref, at, part in split_rows(total.astype(BF), own_ref, other_ref, i):
            ref[at, :] = part


def down_delta_kernel(count, rank, *refs):
    ranks_ref, local_ref = refs[:2]
    factors = refs[2 : 2 + 2 * count]
    own_ref, other_ref = refs[2 + 2 * count :]
    slots = factors[0].shape[0]
    rows = ranks_ref.shape[1]
    width = own_ref.shape[1]
    fan = fan_out(0, rank, rank, slots)
    for i in range(count):
        total = jnp.zeros((rows, width), F32)
        spread = dot(ranks_ref[i], fan)
        for which in range(2):
            mask = slot_mask(local_ref[i], rows, rank, which * slots, slots)
            wide = jnp.where(mask, spread, 0.0).astype(BF)
            factor = factors[2 * i + which]
            factor = factor[:, :, factor.shape[2] - width :].reshape(slots * rank, width)
            total += dot(wide, factor)
        for ref, at, part in split_rows(total.astype(BF), own_ref, other_ref, i):
            ref[at, :] = part


def pack_rows(take_ref, own_ref, other_ref, seated_ref):
    count, rows = seated_ref.shape[:2]
    half = rows // 2

    def pack(i, carry):
        at = pl.ds(pl.multiple_of(i * half, half), half)
        seated_ref[i, :half, :] = dot_bf(take_ref[0, at, :], own_ref[...])
        seated_ref[i, half:, :] = dot_bf(take_ref[1, at, :], other_ref[...])
        return carry

    lax.fori_loop(0, count, pack, 0)


def packing(kernel, count, rank, take_ref, own_ref, other_ref, *refs):
    seated_ref = refs[-1]
    pack_rows(take_ref, own_ref, other_ref, seated_ref)
    kernel(count, rank, seated_ref, *refs[:-1])


def seated_call(kernel, rank, take, pair, local, factors, width, flops):
    count, rows = local.shape[:2]
    out = jax.ShapeDtypeStruct((count * rows // 2, width), BF)
    flat = [f for pair in factors for f in pair]
    moved = sum(2 * f.size for f in flat) + 4 * out.size + 4 * pair[0].size + 2 * take.size
    return pl.pallas_call(
        functools.partial(packing, kernel, count, rank),
        in_specs=[pl.BlockSpec(memory_space=pltpu.VMEM)] * (4 + len(flat)),
        out_specs=[pl.BlockSpec(memory_space=pltpu.VMEM)] * 2,
        out_shape=[out, out],
        scratch_shapes=[pltpu.VMEM((count, rows, pair[0].shape[1]), BF)],
        compiler_params=pltpu.CompilerParams(vmem_limit_bytes=9 << 20),
        cost_estimate=pl.CostEstimate(flops=flops, bytes_accessed=moved, transcendentals=0),
    )(take, *pair, local, *flat)


def layer(
    tokens,
    token_tenant,
    tenant_storage_slot,
    gate_matrix,
    up_matrix,
    down_matrix,
    adapter_gate_up_inputs,
    adapter_gate_up_outputs,
    adapter_down_inputs,
    adapter_down_outputs,
):
    groups = lax.axis_size(GRP)
    rows = tokens.shape[0]
    block_slots = adapter_gate_up_inputs.shape[0]
    rank = adapter_gate_up_inputs.shape[2] // 2
    hidden_share = gate_matrix.shape[1]
    width_share = tokens.shape[1]
    capacity = 2 * rows // groups
    chips = groups // 2
    side = chips * capacity

    in_factors = [(adapter_gate_up_inputs,)]
    in_factors += [(shift(adapter_gate_up_inputs, "z", step),) for step in (1, -1, 2)]
    pieces = gather_tokens(tokens)
    gate_part = adapter_gate_up_outputs[:, :rank, :]
    up_part = adapter_gate_up_outputs[:, rank:, :]
    out_factors = ring(gate_part, up_part)
    down_in = adapter_down_inputs.swapaxes(1, 2)
    half = block_slots // 2
    low = jnp.concatenate([down_in[:half], adapter_down_outputs[:half]], 2)
    high = jnp.concatenate([down_in[half:], adapter_down_outputs[half:]], 2)
    down_factors = ring(low, high)
    base_gate = base_product(pieces, gate_matrix)
    base_up = base_product(pieces, up_matrix)

    tokens_pair = (tokens, swap(tokens))
    tenants = jnp.stack([token_tenant, swap(token_tenant)])
    table = jnp.arange(tenant_storage_slot.shape[0], dtype=jnp.int32)
    match = tenants[:, :, None] == table[None, None, :]
    slot = jnp.sum(jnp.where(match, tenant_storage_slot[None, None, :], 0), 2)
    server = slot // block_slots
    local = slot - server * block_slots
    picks = (server[:, :, None] == jnp.arange(groups, dtype=jnp.int32)).astype(jnp.int32)
    place = jnp.sum(picks * (jnp.cumsum(picks, 1) - 1), 2)
    apart = lax.rem(server // 2 - lax.axis_index("z") + chips, chips)
    turn = jnp.where(apart == 0, 0, jnp.where(apart == chips - 1, 1, jnp.where(apart == 1, 2, 3)))
    seat = turn * capacity + place
    mine = lax.rem(server, 2) == lax.axis_index("c")
    here = jnp.where(mine, seat, -1)
    there = jnp.where(mine, -1, seat)[0]
    seats = jnp.arange(side, dtype=jnp.int32)
    take = (seats[None, :, None] == here[:, None, :]).astype(BF)
    give_here = (here[0][:, None] == seats[None, :]).astype(BF)
    give_there = (there[:, None] == seats[None, :]).astype(BF)
    give = jnp.concatenate([give_here, give_there], 1)

    def by_block(pair):
        packed = [dot_bf(take[g], v).reshape(chips, capacity, -1) for g, v in enumerate(pair)]
        return jnp.concatenate(packed, 1)

    def home(own, other):
        return dot(give, jnp.concatenate([own, other], 0))

    seat_local = by_block((local[0][:, None].astype(BF), local[1][:, None].astype(BF)))

    flops = 8 * side * block_slots * rank * width_share
    own, other = seated_call(
        in_rank_kernel, rank, take, tokens_pair, seat_local, in_factors, 2 * rank, flops
    )
    home_part = home(own, swap(other)).astype(BF)
    ranks = sum_tp(home_part)
    ranks_pair = (ranks, swap(ranks))

    flops = 8 * side * block_slots * rank * hidden_share
    own, other = seated_call(
        delta_kernel, rank, take, ranks_pair, seat_local, out_factors, 2 * hidden_share, flops
    )
    other = swap(other)
    hidden = hidden_rows(give_here, give_there, own, other, base_gate, base_up)

    partial = down_product(hidden, down_matrix, lax.axis_size("x"))
    hidden_pair = (hidden, swap(hidden))
    summed = scatter_sum(partial)

    flops = 4 * side * block_slots * rank * hidden_share
    own, other = seated_call(
        down_rank_kernel, rank, take, hidden_pair, seat_local, down_factors, rank, flops
    )
    down_rows = home(own, swap(other)).astype(BF)
    down_ranks = sum_tp(down_rows)
    down_pair = (down_ranks, swap(down_ranks))
    flops = 4 * side * block_slots * rank * width_share
    own, other = seated_call(
        down_delta_kernel, rank, take, down_pair, seat_local, down_factors, width_share, flops
    )
    returned = home(own, swap(other))
    return (summed + returned).astype(BF)


def solution(mesh):
    sizes = mesh.devices.shape
    cores = 2
    side = 4
    fine = Mesh(
        mesh.devices.reshape(sizes[0] // cores, cores, sizes[1] // side, side),
        ("z", "c", "x", "y"),
    )
    return jax.shard_map(
        layer,
        mesh=fine,
        in_specs=(
            P(GRP, TP),
            P(GRP),
            P(),
            P(None, TP),
            P(None, TP),
            P(TP, None),
            P(GRP, TP, None),
            P(GRP, None, TP),
            P(GRP, TP, None),
            P(GRP, None, TP),
        ),
        out_specs=P(GRP, TP),
        check_vma=False,
    )
```
